128 devices in a mesh: blk: 16 (over x_lo, y, core), feat: 8 (over z, x_hi).
Axes of the slice: x: 4 (x_hi: 2, x_lo: 2; x = x_hi * 2 + x_lo), y: 4, z: 4, core: 2. Of those that a mesh axis runs over, the one named last changes fastest.
Arguments:
- features: bfloat16 [256, 32768], P('feat', 'blk'), may hold values from -6 to 6
- adj_tiles: bfloat16 [16, 8, 16, 48, 128, 128], P('blk', 'feat'), may hold values from -0.02734375 to 0.02734375
- tile_rows: int32 [16, 8, 16, 48], P('blk', 'feat'), may hold values from 0 to 15
- tile_cols: int32 [16, 8, 16, 48], P('blk', 'feat'), may hold values from 0 to 15
- counts: int32 [16, 8, 16], P('blk', 'feat'), may hold values from 1 to 48, as said below
- weight: bfloat16 [256, 256], replicated, may hold values from -0.375 to 0.375
- cotangent: bfloat16 [256, 32768], P(None, ('blk', 'feat')), may hold values from -6 to 6
Outputs:
- activated: bfloat16 [256, 32768], P(None, ('blk', 'feat'))
- weight_grad: float32 [256, 256], P('feat')
The draws below stay inside these ranges and needn't reach their ends.
Inputs may be any that keep to these rules, and one draw needn't show every extreme that they name: Only the first counts slots of a partition, group and source partition are live; the slots a partition takes from its own nodes are all live in every group.
All inputs are finite; a program needn't handle non-finite values.
Results may differ from the reference program's by a relative error of at most 0.02.
Values may be sent and summed in bfloat16 or wider, within the bound.
A program may use at most 320 MiB of HBM per device.

```python
import math
import jax
import jax.numpy as jnp
from jax import lax

F = 256
TILE = 128
ROWS = 2048
CAPF = 48
NODES = 32768
N_BLK = 16
N_FEAT = 8


def draw_counts(key, part):
    first_key, second_key = jax.random.split(jax.random.fold_in(key, 11))
    level_pick = jax.random.randint(first_key, (N_BLK, 1, 1), 0, 4)
    levels = jnp.array([1, 2, 4, 8], dtype=jnp.int32)
    level_val = jnp.take(levels, level_pick)
    base_val = jax.random.randint(second_key, (N_BLK, N_FEAT, N_BLK), 1, CAPF + 1)
    counts_val = jnp.clip(base_val * level_val // 8, 1, CAPF)
    own_part = jnp.arange(N_BLK)[:, None, None] == jnp.arange(N_BLK)[None, None, :]
    return jnp.where(own_part, CAPF, counts_val).astype(jnp.int32)


def plant(values, own_key, low, top_value):
    dims = values.shape
    place = [jax.random.randint(jax.random.fold_in(own_key, axis), (), 0, dims[axis]) for axis in range(len(dims))]
    values = values.at[tuple(place)].set(low)
    longest = dims.index(max(dims))
    place[longest] = (place[longest] + 1) % dims[longest]
    return values.at[tuple(place)].set(top_value)


def shard_levels(key, dims, cuts, least, largest):
    factor_of, own = 1.0, jax.random.fold_in(key, 6)
    for dim, shards_of in cuts:
        steps = jnp.exp(jax.random.uniform(jax.random.fold_in(own, dim), (shards_of,), jnp.float32, least / len(cuts), largest / len(cuts)))
        factor_of = factor_of * jnp.repeat(steps, dims[dim] // shards_of).reshape([-1 if axis == dim else 1 for axis in range(len(dims))])
    return factor_of


def scatter_about(own_key, shape, width, limit, pieces=(), kind=jnp.bfloat16):
    factor_of = shard_levels(own_key, shape, pieces, -0.22, 0.18) if pieces else 1.0
    result = jax.random.normal(own_key, shape, jnp.float32) * width * factor_of
    return jnp.minimum(jnp.maximum(result, -limit), limit).astype(kind)


def setup_inputs(seed: int = 0) -> dict:
    arg_keys = jax.random.split(jax.random.key(seed), 8)
    features = scatter_about(arg_keys[0], (F, NODES), 1.0, 6.0, ((0, 8), (1, 16)))
    adj_tiles = scatter_about(arg_keys[1], (N_BLK, N_FEAT, N_BLK, CAPF, TILE, TILE), (TILE * N_BLK * N_FEAT * CAPF // (ROWS // TILE)) ** -0.5, 0.02734375, ((0, 16), (1, 8)))
    tile_rows = plant(jax.random.randint(arg_keys[2], (N_BLK, N_FEAT, N_BLK, CAPF), 0, ROWS // TILE), jax.random.fold_in(arg_keys[2], 1), 0, (ROWS // TILE) - 1).astype(jnp.int32)
    tile_cols = plant(jax.random.randint(arg_keys[3], (N_BLK, N_FEAT, N_BLK, CAPF), 0, ROWS // TILE), jax.random.fold_in(arg_keys[3], 1), 0, (ROWS // TILE) - 1).astype(jnp.int32)
    counts = draw_counts(jax.random.fold_in(arg_keys[7], 71), 0)
    weight = scatter_about(arg_keys[5], (F, F), F ** -0.5, 0.375)
    cotangent = scatter_about(arg_keys[6], (F, NODES), 1.0, 6.0, ((1, 128),))
    return {"features": features, "adj_tiles": adj_tiles, "tile_rows": tile_rows, "tile_cols": tile_cols, "counts": counts, "weight": weight, "cotangent": cotangent}


def partition_terms(part_index, features, adj_tiles, tile_rows, tile_cols, counts):
    row_tiles = ROWS // TILE
    col_panels = features.reshape(F, N_BLK * row_tiles, TILE)
    sources = jnp.arange(N_BLK, dtype=jnp.int32)
    slot_index = jnp.arange(CAPF, dtype=jnp.int32)
    tile_range = jnp.arange(row_tiles, dtype=jnp.int32)

    def add_group(group_idx, running):
        block = adj_tiles[part_index, group_idx].reshape(N_BLK * CAPF, TILE, TILE)
        rows_here = tile_rows[part_index, group_idx].reshape(-1).astype(jnp.int32)
        cols_here = (sources[:, None] * row_tiles + tile_cols[part_index, group_idx].astype(jnp.int32)).reshape(-1)
        live_mask = (slot_index[None, :] < counts[part_index, group_idx][:, None]).reshape(-1)
        gathered = jnp.take(col_panels, cols_here, axis=1)
        products = jnp.einsum('kij,fkj->fki', block.astype(jnp.float32), gathered.astype(jnp.float32), precision=lax.Precision.HIGHEST)
        placing = ((rows_here[:, None] == tile_range[None, :]) & live_mask[:, None]).astype(jnp.float32)
        summed = jnp.einsum('fki,kr->fri', products, placing, precision=lax.Precision.HIGHEST)
        return running + summed.reshape(F, ROWS)
    return lax.fori_loop(0, N_FEAT, add_group, jnp.zeros((F, ROWS), jnp.float32))

def reference(features, adj_tiles, tile_rows, tile_cols, counts, weight, cotangent):
    per_part = lax.map(lambda part_index: partition_terms(part_index, features, adj_tiles, tile_rows, tile_cols, counts), jnp.arange(N_BLK, dtype=jnp.int32))
    aggregated = jnp.transpose(per_part, (1, 0, 2)).reshape(F, NODES).astype(jnp.bfloat16)
    preact = jnp.dot(weight, aggregated, preferred_element_type=jnp.float32)
    activated = (preact * jax.nn.sigmoid(preact)).astype(jnp.bfloat16)
    sigmoid_z = jax.nn.sigmoid(preact)
    slope = (cotangent.astype(jnp.float32) * sigmoid_z * (1.0 + preact * (1.0 - sigmoid_z))).astype(jnp.bfloat16)
    weight_grad = lax.dot_general(slope, aggregated, (((1,), (1,)), ((), ())), preferred_element_type=jnp.float32)
    weight_grad = weight_grad * (1.0 / math.sqrt(NODES))
    return (activated, weight_grad)
```

```python
import functools
import math

import jax
import jax.numpy as jnp
from jax import lax
from jax.experimental import pallas as pl
from jax.experimental.pallas import tpu as pltpu
from jax.sharding import PartitionSpec as P

MESH = pl.DeviceIdType.MESH
TILE = 128
ORDERS = (("x", "y", "z"), ("y", "z", "x"), ("z", "x", "y"))
COLUMNS = ((0, 3, 6), (6, 8, 11), (11, 14, 16))
MIB = 2**20


def place():
    blk = lax.axis_index("blk")
    feat = lax.axis_index("feat")
    return {
        "x": (feat % 2) * 2 + blk // 8,
        "y": (blk // 2) % 4,
        "z": feat // 2,
        "c": blk % 2,
    }


def device(at):
    return {
        "blk": ((at["x"] % 2) * 4 + at["y"]) * 2 + at["c"],
        "feat": at["z"] * 2 + at["x"] // 2,
    }


def moved(at, dim, by):
    return {**at, dim: (at[dim] + by) % (2 if dim == "c" else 4)}


class Sender:
    def __init__(self, send_sem, recv_sem):
        self.send_sem, self.recv_sem, self.used = send_sem, recv_sem, 0
        self.all = []

    def start(self, ref, to):
        i = self.used
        self.used += 1
        copy = pltpu.make_async_remote_copy(
            src_ref=ref,
            dst_ref=ref,
            send_sem=self.send_sem.at[i],
            recv_sem=self.recv_sem.at[i],
            device_id=device(to),
            device_id_type=MESH,
        )
        self.all.append(copy)
        copy.start()
        return copy


N_COPIES = 3 * 24


def gather_kernel(x_ref, full, own_sem, send_sem, recv_sem):
    me = place()
    sibling = moved(me, "c", 1)
    neighbours = [moved(me, d, by) for d in "xyz" for by in (1, 3)] + [sibling]

    def region(at, lo, hi):
        def index(value):
            if value is None:
                return slice(None)
            if isinstance(value, tuple):
                return slice(2 * value[1], 2 * value[1] + 2)
            return pl.ds(value, 1)

        x = at["x"]
        if x is None:
            x_lo, x_hi = slice(None), slice(None)
        elif isinstance(x, tuple):
            x_lo, x_hi = slice(None), pl.ds(x[1], 1)
        else:
            x_lo, x_hi = pl.ds(x % 2, 1), pl.ds(x // 2, 1)
        return full.at[
            x_lo, index(at["y"]), pl.ds(me["c"], 1), lo:hi, index(at["z"]), x_hi
        ]

    barrier = pltpu.get_barrier_semaphore()
    for other in neighbours:
        pl.semaphore_signal(barrier, inc=1, device_id=device(other), device_id_type=MESH)
    own = []
    for ct in range(16):
        own.append(
            pltpu.make_async_copy(
                x_ref.at[:, ct * TILE : (ct + 1) * TILE],
                full.at[me["x"] % 2, me["y"], me["c"], ct, me["z"], me["x"] // 2],
                own_sem.at[ct],
            )
        )
        own[-1].start()
    for copy in own:
        copy.wait()
    pl.semaphore_wait(barrier, len(neighbours))

    net = Sender(send_sem, recv_sem)
    passed = []
    state = [{} for _ in ORDERS]
    for (d1, d2, d3), (lo, mid, hi), st in zip(ORDERS, COLUMNS, state):
        st["a"] = net.start(region(me, lo, hi), moved(me, d1, 1))
        st["b"] = net.start(region(me, lo, hi), moved(me, d1, 3))
    for (d1, d2, d3), (lo, mid, hi), st in zip(ORDERS, COLUMNS, state):
        st["a"].wait_recv()
        st["ah"] = net.start(region(moved(me, d1, 3), lo, mid), moved(me, d1, 1))
        st["b"].wait_recv()
        st["bh"] = net.start(region(moved(me, d1, 1), mid, hi), moved(me, d1, 3))
    for stage in (2, 3):
        for (d1, d2, d3), (lo, mid, hi), st in zip(ORDERS, COLUMNS, state):
            inner, ring = (d1, d2) if stage == 2 else (d2, d3)
            held = {**me, d1: None}
            if stage == 3:
                held[d2] = None
            if stage == 2:
                st["ah"].wait_recv()
                st["bh"].wait_recv()
            else:
                for name in ("p1", "m0", "pf", "mf"):
                    st[name].wait_recv()
                passed.append(net.start(region(held, lo, hi), sibling))
            for name, by, half in (("p0", 1, 0), ("m1", 3, 1), ("p1", 1, 1), ("m0", 3, 0)):
                st[name] = net.start(
                    region({**held, inner: ("h", half)}, lo, hi), moved(me, ring, by)
                )
            st["held"], st["inner"], st["ring"] = held, inner, ring

        def came(st, by, half):
            return {**moved(st["held"], st["ring"], by), st["inner"]: ("h", half)}

        for (lo, mid, hi), st in zip(COLUMNS, state):
            st["p0"].wait_recv()
            st["pf"] = net.start(region(came(st, 3, 0), lo, hi), moved(me, st["ring"], 1))
            if stage == 3:
                passed.append(net.start(region(came(st, 3, 0), lo, hi), sibling))
            st["m1"].wait_recv()
            st["mf"] = net.start(region(came(st, 1, 1), lo, hi), moved(me, st["ring"], 3))
            if stage == 3:
                passed.append(net.start(region(came(st, 1, 1), lo, hi), sibling))
    for name, by, half in (("p1", 3, 1), ("m0", 1, 0), ("pf", 2, 0), ("mf", 2, 1)):
        for (lo, mid, hi), st in zip(COLUMNS, state):
            st[name].wait_recv()
            passed.append(net.start(region(came(st, by, half), lo, hi), sibling))
    for copy in passed:
        copy.wait_recv()
    for copy in net.all:
        copy.wait_send()


def gather(features):
    return pl.pallas_call(
        gather_kernel,
        out_shape=jax.ShapeDtypeStruct((2, 4, 2, 16, 4, 2, 32, TILE), jnp.bfloat16),
        in_specs=[pl.BlockSpec(memory_space=pl.ANY)],
        out_specs=pl.BlockSpec(memory_space=pl.ANY),
        scratch_shapes=[
            pltpu.SemaphoreType.DMA((16,)),
            pltpu.SemaphoreType.DMA((N_COPIES,)),
            pltpu.SemaphoreType.DMA((N_COPIES,)),
        ],
        compiler_params=pltpu.CompilerParams(collective_id=0, has_side_effects=True),
        name="gather",
    )(features)


CHUNK = 16


def aggregate_kernel(
    rows_ref, cols_ref, counts_ref, full_hbm, tiles_hbm, out_ref, full, tiles, total, fsem, tsem
):
    sources, slots = tiles_hbm.shape[:2]

    def full_copy(s):
        return pltpu.make_async_copy(full_hbm.at[s], full.at[s], fsem.at[s])

    def chunk_copy(s, c):
        part = pl.ds(c * CHUNK, CHUNK)
        return pltpu.make_async_copy(
            tiles_hbm.at[s, part], tiles.at[s, part], tsem.at[s, c]
        )

    def over_chunks(s, act):
        for c in range(slots // CHUNK):
            pl.when(counts_ref[s] > c * CHUNK)(lambda c=c: act(chunk_copy(s, c)))

    @pl.loop(0, sources)
    def _(s):
        full_copy(s).start()
        over_chunks(s, lambda copy: copy.start())

    total[...] = jnp.zeros_like(total)

    @pl.loop(0, sources)
    def _(s):
        full_copy(s).wait()
        over_chunks(s, lambda copy: copy.wait())

        @pl.loop(0, counts_ref[s])
        def _(k):
            at = pl.ds(pl.multiple_of(rows_ref[s, k] * TILE, TILE), TILE)
            total[at, :] += lax.dot_general(
                tiles[s, k],
                full[s, cols_ref[s, k]],
                (((1,), (1,)), ((), ())),
                preferred_element_type=jnp.float32,
            )

    out_ref[...] = total[...].astype(out_ref.dtype)


def aggregate(rows, cols, counts, full, tiles):
    sources, slots = tiles.shape[:2]
    smem = pl.BlockSpec(memory_space=pltpu.SMEM)
    hbm = pl.BlockSpec(memory_space=pl.ANY)
    return pl.pallas_call(
        aggregate_kernel,
        out_shape=jax.ShapeDtypeStruct((2048, 256), jnp.bfloat16),
        in_specs=[smem, smem, smem, hbm, hbm],
        out_specs=pl.BlockSpec(memory_space=pltpu.VMEM),
        scratch_shapes=[
            pltpu.VMEM(full.shape, jnp.bfloat16),
            pltpu.VMEM(tiles.shape, jnp.bfloat16),
            pltpu.VMEM((2048, 256), jnp.float32),
            pltpu.SemaphoreType.DMA((sources,)),
            pltpu.SemaphoreType.DMA((sources, slots // CHUNK)),
        ],
        compiler_params=pltpu.CompilerParams(vmem_limit_bytes=58 * MIB),
        name="aggregate",
    )(rows, cols, counts, full, tiles)


def tail_kernel(
    part, weight, cotangent, act_ref, grad_ref,
    held, terms, terms_in, mine, mine_in, done,
    psem, pin, tsem, tin, msem, min_, dsem, din,
):
    blk, feat = lax.axis_index("blk"), lax.axis_index("feat")
    chip, core = blk // 2, blk % 2
    barrier = pltpu.get_barrier_semaphore()
    for i in range(1, 8):
        pl.semaphore_signal(
            barrier, inc=1, device_id={"feat": (feat + i) % 8}, device_id_type=MESH
        )
    for i in range(1, 16):
        pl.semaphore_signal(
            barrier, inc=1, device_id={"blk": (blk + i) % 16}, device_id_type=MESH
        )
    pl.semaphore_wait(barrier, 22)

    def remote(src, dst, send, recv, to):
        copy = pltpu.make_async_remote_copy(
            src_ref=src, dst_ref=dst, send_sem=send, recv_sem=recv,
            device_id=to, device_id_type=MESH,
        )
        copy.start()
        return copy

    sent = []
    for i in range(1, 8):
        to = (feat + i) % 8
        sent.append(
            remote(part.at[to], held.at[i - 1], psem.at[i - 1], pin.at[i - 1], {"feat": to})
        )
    summed = part[feat].astype(jnp.float32)
    for i in range(7):
        sent[i].wait_recv()
        summed = summed + held[i].astype(jnp.float32)
    nodes = summed.astype(jnp.bfloat16)
    preact = lax.dot_general(
        weight[...], nodes, (((1,), (1,)), ((), ())), preferred_element_type=jnp.float32
    )
    sigmoid = jax.nn.sigmoid(preact)
    act_ref[...] = (preact * sigmoid).astype(jnp.bfloat16)
    slope = cotangent[...].astype(jnp.float32) * sigmoid * (1.0 + preact * (1.0 - sigmoid))
    local = jnp.dot(slope.astype(jnp.bfloat16), nodes, preferred_element_type=jnp.float32)
    terms[...] = local.reshape(terms.shape)
    sent_terms = []
    for i in range(1, 8):
        to = (feat + i) % 8
        sent_terms.append(
            remote(terms.at[to], terms_in.at[i - 1], tsem.at[i - 1], tin.at[i - 1], {"feat": to})
        )
    share = terms[feat]
    for i in range(7):
        sent_terms[i].wait_recv()
        share = share + terms_in[i]
    for q in range(8):
        r, c = q // 2 * 8, q % 2 * 128
        mine[q] = share[r : r + 8, c : c + 128]
    sent_mine = []
    for i in range(1, 16):
        to = (blk + i) % 16
        sent_mine.append(
            remote(mine.at[to // 2], mine_in.at[i - 1], msem.at[i - 1], min_.at[i - 1], {"blk": to})
        )
    piece = mine[chip]
    for i in range(15):
        sent_mine[i].wait_recv()
        piece = piece + mine_in[i]
    done[chip] = piece * (1.0 / math.sqrt(32768))
    sent_done = []
    for i in range(1, 8):
        to = (chip + i) % 8 * 2 + core
        sent_done.append(
            remote(done.at[chip], done.at[chip], dsem.at[i - 1], din.at[i - 1], {"blk": to})
        )
    for copy in sent_done:
        copy.wait_recv()
    for q in range(8):
        r, c = q // 2 * 8, q % 2 * 128
        grad_ref[r : r + 8, c : c + 128] = done[q]
    for copy in sent + sent_terms + sent_mine + sent_done:
        copy.wait_send()


def tail(part, weight, cotangent):
    vmem = pl.BlockSpec(memory_space=pltpu.VMEM)
    dma = pltpu.SemaphoreType.DMA
    return pl.pallas_call(
        tail_kernel,
        out_shape=(
            jax.ShapeDtypeStruct((256, 256), jnp.bfloat16),
            jax.ShapeDtypeStruct((32, 256), jnp.float32),
        ),
        in_specs=[vmem] * 3,
        out_specs=(vmem, vmem),
        scratch_shapes=[
            pltpu.VMEM((7, 256, 256), jnp.bfloat16),
            pltpu.VMEM((8, 32, 256), jnp.float32),
            pltpu.VMEM((7, 32, 256), jnp.float32),
            pltpu.VMEM((8, 8, 128), jnp.float32),
            pltpu.VMEM((15, 8, 128), jnp.float32),
            pltpu.VMEM((8, 8, 128), jnp.float32),
            dma((7,)), dma((7,)), dma((7,)), dma((7,)),
            dma((15,)), dma((15,)), dma((7,)), dma((7,)),
        ],
        compiler_params=pltpu.CompilerParams(collective_id=1, has_side_effects=True),
        name="tail",
    )(part, weight, cotangent)


def shards(features, adj_tiles, tile_rows, tile_cols, counts, weight, cotangent):
    sources, slots = adj_tiles.shape[2:4]
    tiles = adj_tiles.reshape(sources, slots, TILE, TILE)
    full = gather(features).reshape(sources, 16, 256, TILE)
    part = aggregate(
        tile_rows.reshape(sources, slots),
        tile_cols.reshape(sources, slots),
        counts.reshape(sources),
        full,
        tiles,
    )
    return tail(part.reshape(8, 256, 256), weight, cotangent)


def solution(mesh):
    in_specs = (
        P("feat", "blk"),
        P("blk", "feat", None, None, None, None),
        P("blk", "feat", None, None),
        P("blk", "feat", None, None),
        P("blk", "feat", None),
        P(),
        P(None, ("blk", "feat")),
    )
    out_specs = (P(None, ("blk", "feat")), P("feat", None))
    return jax.shard_map(shards, mesh=mesh, in_specs=in_specs, out_specs=out_specs, check_vma=False)
```

```python
import functools
import math

import jax
import jax.numpy as jnp
from jax import lax
from jax.experimental import pallas as pl
from jax.experimental.pallas import tpu as pltpu
from jax.sharding import PartitionSpec as P

MESH = pl.DeviceIdType.MESH
TILE = 128
ORDERS = (("x", "y", "z"), ("y", "z", "x"), ("z", "x", "y"))
CHUNKS = (
    ((0, 2), (6, 8), (11, 13)),
    ((2, 4), (8, 10), (13, 15)),
    ((4, 6), (10, 11), (15, 16)),
)
MIB = 2**20


def place():
    blk = lax.axis_index("blk")
    feat = lax.axis_index("feat")
    return {
        "x": (feat % 2) * 2 + blk // 8,
        "y": (blk // 2) % 4,
        "z": feat // 2,
        "c": blk % 2,
    }


def device(at):
    return {
        "blk": ((at["x"] % 2) * 4 + at["y"]) * 2 + at["c"],
        "feat": at["z"] * 2 + at["x"] // 2,
    }


def moved(at, dim, by):
    return {**at, dim: (at[dim] + by) % (2 if dim == "c" else 4)}


class Sender:
    def __init__(self, send_sem, recv_sem):
        self.send_sem, self.recv_sem, self.used = send_sem, recv_sem, 0
        self.all = []

    def start(self, ref, to):
        i = self.used
        self.used += 1
        copy = pltpu.make_async_remote_copy(
            src_ref=ref,
            dst_ref=ref,
            send_sem=self.send_sem.at[i],
            recv_sem=self.recv_sem.at[i],
            device_id=device(to),
            device_id_type=MESH,
        )
        self.all.append(copy)
        copy.start()
        return copy


N_COPIES = 9 * 21


def gather_kernel(x_ref, full, own_sem, send_sem, recv_sem):
    me = place()
    sibling = moved(me, "c", 1)
    neighbours = [moved(me, d, by) for d in "xyz" for by in (1, 3)] + [sibling]

    def region(at, span, rows=slice(None)):
        def index(value):
            if value is None:
                return slice(None)
            if isinstance(value, tuple):
                return slice(2 * value[1], 2 * value[1] + 2)
            return pl.ds(value, 1)

        x = at["x"]
        if x is None:
            x_lo, x_hi = slice(None), slice(None)
        elif isinstance(x, tuple):
            x_lo, x_hi = slice(None), pl.ds(x[1], 1)
        else:
            x_lo, x_hi = pl.ds(x % 2, 1), pl.ds(x // 2, 1)
        return full.at[
            x_lo, index(at["y"]), pl.ds(me["c"], 1), slice(*span), index(at["z"]), x_hi, rows
        ]

    barrier = pltpu.get_barrier_semaphore()
    for other in neighbours:
        pl.semaphore_signal(barrier, inc=1, device_id=device(other), device_id_type=MESH)
    own = []
    for ct in range(16):
        own.append(
            pltpu.make_async_copy(
                x_ref.at[:, ct * TILE : (ct + 1) * TILE],
                full.at[me["x"] % 2, me["y"], me["c"], ct, me["z"], me["x"] // 2],
                own_sem.at[ct],
            )
        )
        own[-1].start()
    for copy in own:
        copy.wait()
    pl.semaphore_wait(barrier, len(neighbours))

    net = Sender(send_sem, recv_sem)
    passed = []
    lower, upper = slice(0, 16), slice(16, 32)
    jobs = [[(order, span, {}) for order, span in zip(ORDERS, spans)] for spans in CHUNKS]

    def to_sibling(at, span):
        passed.append(net.start(region(at, span), sibling))

    def open_ring(held, inner, ring, span, st):
        for name, by, half in (("p0", 1, 0), ("m1", 3, 1), ("p1", 1, 1), ("m0", 3, 0)):
            st[name] = net.start(region({**held, inner: ("h", half)}, span), moved(me, ring, by))

    def pass_on(held, inner, ring, span, st):
        st["p0"].wait_recv()
        at = {**moved(held, ring, 3), inner: ("h", 0)}
        st["pf"] = net.start(region(at, span), moved(me, ring, 1))
        st["m1"].wait_recv()
        at = {**moved(held, ring, 1), inner: ("h", 1)}
        st["mf"] = net.start(region(at, span), moved(me, ring, 3))

    for chunk in jobs:
        for (d1, d2, d3), span, st in chunk:
            st["a"] = net.start(region(me, span), moved(me, d1, 1))
            st["b"] = net.start(region(me, span), moved(me, d1, 3))
    for chunk in jobs:
        for (d1, d2, d3), span, st in chunk:
            st["a"].wait_recv()
            st["ah"] = net.start(region(moved(me, d1, 3), span, lower), moved(me, d1, 1))
            st["b"].wait_recv()
            st["bh"] = net.start(region(moved(me, d1, 1), span, upper), moved(me, d1, 3))
    for chunk in jobs:
        for (d1, d2, d3), span, st in chunk:
            st["ah"].wait_recv()
            st["bh"].wait_recv()
            open_ring({**me, d1: None}, d1, d2, span, st)
    for chunk in jobs:
        for (d1, d2, d3), span, st in chunk:
            pass_on({**me, d1: None}, d1, d2, span, st)
        for (d1, d2, d3), span, st in chunk:
            for name in ("p1", "m0", "pf", "mf"):
                st[name].wait_recv()
            plane = {**me, d1: None, d2: None}
            open_ring(plane, d2, d3, span, st)
            to_sibling(plane, span)
    for chunk in jobs:
        for (d1, d2, d3), span, st in chunk:
            pass_on({**me, d1: None, d2: None}, d2, d3, span, st)
    for chunk in jobs:
        for name, by in (("p1", 3), ("m0", 1)):
            for (d1, d2, d3), span, st in chunk:
                st[name].wait_recv()
                to_sibling(moved({**me, d1: None, d2: None}, d3, by), span)
        for name, half in (("pf", 0), ("mf", 1)):
            for (d1, d2, d3), span, st in chunk:
                st[name].wait_recv()
                at = moved({**me, d1: None, d2: None}, d3, 2)
                to_sibling({**at, d2: ("h", half)}, span)
    for copy in passed:
        copy.wait_recv()
    for copy in net.all:
        copy.wait_send()


def gather(features):
    return pl.pallas_call(
        gather_kernel,
        out_shape=jax.ShapeDtypeStruct((2, 4, 2, 16, 4, 2, 32, TILE), jnp.bfloat16),
        in_specs=[pl.BlockSpec(memory_space=pl.ANY)],
        out_specs=pl.BlockSpec(memory_space=pl.ANY),
        scratch_shapes=[
            pltpu.SemaphoreType.DMA((16,)),
            pltpu.SemaphoreType.DMA((N_COPIES,)),
            pltpu.SemaphoreType.DMA((N_COPIES,)),
        ],
        compiler_params=pltpu.CompilerParams(collective_id=0, has_side_effects=True),
        name="gather",
    )(features)


SLOTS = 16
GROUP = 4
BATCH = 32


def aggregate_kernel(
    rows_ref, cols_ref, counts_ref, full_hbm, tiles_hbm, out_ref,
    full, tiles, total, listed, fsem, tsem,
):
    sources = counts_ref.shape[0]
    slots = tiles_hbm.shape[0] // sources

    def full_copy(s):
        return pltpu.make_async_copy(full_hbm.at[s], full.at[s], fsem.at[s])

    def tile_copies(s, act):
        for c in range(slots // SLOTS):
            part = pl.ds(s * slots + c * SLOTS, SLOTS)
            copy = pltpu.make_async_copy(tiles_hbm.at[part], tiles.at[part], tsem.at[s, c])
            pl.when(counts_ref[s] > c * SLOTS)(lambda copy=copy: act(copy))

    @pl.loop(0, sources)
    def _(s):
        full_copy(s).start()
        tile_copies(s, lambda copy: copy.start())

    total[...] = jnp.zeros_like(total)
    none = sources * slots
    tiles[none] = jnp.zeros(tiles.shape[1:], tiles.dtype)

    @pl.loop(0, sources // GROUP)
    def _(g):
        end = 0
        for i in range(GROUP):
            s = g * GROUP + i

            def enter(j, carry, s=s, end=end):
                for u in range(8):
                    k = j * 8 + u
                    code = (s * slots + k) * 4096 + (s * 16 + cols_ref[s, k]) * 16 + rows_ref[s, k]
                    listed[end + k] = code
                return carry

            lax.fori_loop(0, (counts_ref[s] + 7) // 8, enter, 0)
            end = end + counts_ref[s]
        for u in range(BATCH):
            listed[end + u] = none * 4096 + g * (GROUP * 16 * 16)
        for i in range(GROUP):
            s = g * GROUP + i
            full_copy(s).wait()
            tile_copies(s, lambda copy: copy.wait())

        @pl.loop(0, (end + BATCH - 1) // BATCH)
        def _(b):
            codes = [listed[b * BATCH + u] for u in range(BATCH)]
            products = [
                lax.dot_general(
                    full[(code >> 8) & 15, (code >> 4) & 15],
                    tiles[code >> 12],
                    (((1,), (1,)), ((), ())),
                    preferred_element_type=jnp.float32,
                )
                for code in codes
            ]
            for code, product in zip(codes, products):
                total[code & 15] += product

    out_ref[...] = total[...].astype(out_ref.dtype)


def aggregate(rows, cols, counts, full, tiles):
    sources, slots = rows.shape
    smem = pl.BlockSpec(memory_space=pltpu.SMEM)
    hbm = pl.BlockSpec(memory_space=pl.ANY)
    return pl.pallas_call(
        aggregate_kernel,
        out_shape=jax.ShapeDtypeStruct((16, 256, TILE), jnp.bfloat16),
        in_specs=[smem, smem, smem, hbm, hbm],
        out_specs=pl.BlockSpec(memory_space=pltpu.VMEM),
        scratch_shapes=[
            pltpu.VMEM((sources, 16, 256, TILE), jnp.bfloat16),
            pltpu.VMEM((sources * slots + 1, TILE, TILE), jnp.bfloat16),
            pltpu.VMEM((16, 256, TILE), jnp.float32),
            pltpu.SMEM((GROUP * slots + BATCH + 8,), jnp.int32),
            pltpu.SemaphoreType.DMA((sources,)),
            pltpu.SemaphoreType.DMA((sources, slots // SLOTS)),
        ],
        compiler_params=pltpu.CompilerParams(vmem_limit_bytes=58 * MIB),
        name="aggregate",
    )(rows, cols, counts, full, tiles)


def tail_kernel(
    part, weight, cotangent, act_ref, grad_ref,
    held, terms, terms_in, mine, mine_in, done,
    psem, pin, tsem, tin, msem, min_, dsem, din,
):
    blk, feat = lax.axis_index("blk"), lax.axis_index("feat")
    chip, core = blk // 2, blk % 2
    barrier = pltpu.get_barrier_semaphore()
    for i in range(1, 8):
        pl.semaphore_signal(
            barrier, inc=1, device_id={"feat": (feat + i) % 8}, device_id_type=MESH
        )
    for i in range(1, 16):
        pl.semaphore_signal(
            barrier, inc=1, device_id={"blk": (blk + i) % 16}, device_id_type=MESH
        )
    pl.semaphore_wait(barrier, 22)

    def remote(src, dst, send, recv, to):
        copy = pltpu.make_async_remote_copy(
            src_ref=src, dst_ref=dst, send_sem=send, recv_sem=recv,
            device_id=to, device_id_type=MESH,
        )
        copy.start()
        return copy

    sent = []
    for i in range(1, 8):
        to = (feat + i) % 8
        sent.append(
            remote(part.at[to], held.at[i - 1], psem.at[i - 1], pin.at[i - 1], {"feat": to})
        )
    summed = part[feat].astype(jnp.float32)
    for i in range(7):
        sent[i].wait_recv()
        summed = summed + held[i].astype(jnp.float32)
    nodes = summed.astype(jnp.bfloat16)
    nodes = jnp.concatenate([nodes[0], nodes[1]], axis=1)
    preact = jnp.dot(weight[...], nodes, preferred_element_type=jnp.float32)
    sigmoid = jax.nn.sigmoid(preact)
    act_ref[...] = (preact * sigmoid).astype(jnp.bfloat16)
    slope = cotangent[...].astype(jnp.float32) * sigmoid * (1.0 + preact * (1.0 - sigmoid))
    local = lax.dot_general(
        slope.astype(jnp.bfloat16),
        nodes,
        (((1,), (1,)), ((), ())),
        preferred_element_type=jnp.float32,
    )
    terms[...] = local.reshape(terms.shape)
    sent_terms = []
    for i in range(1, 8):
        to = (feat + i) % 8
        sent_terms.append(
            remote(terms.at[to], terms_in.at[i - 1], tsem.at[i - 1], tin.at[i - 1], {"feat": to})
        )
    share = terms[feat]
    for i in range(7):
        sent_terms[i].wait_recv()
        share = share + terms_in[i]
    for q in range(8):
        r, c = q // 2 * 8, q % 2 * 128
        mine[q] = share[r : r + 8, c : c + 128]
    sent_mine = []
    for i in range(1, 16):
        to = (blk + i) % 16
        sent_mine.append(
            remote(mine.at[to // 2], mine_in.at[i - 1], msem.at[i - 1], min_.at[i - 1], {"blk": to})
        )
    piece = mine[chip]
    for i in range(15):
        sent_mine[i].wait_recv()
        piece = piece + mine_in[i]
    done[chip] = piece * (1.0 / math.sqrt(32768))
    sent_done = []
    for i in range(1, 8):
        to = (chip + i) % 8 * 2 + core
        sent_done.append(
            remote(done.at[chip], done.at[chip], dsem.at[i - 1], din.at[i - 1], {"blk": to})
        )
    for copy in sent_done:
        copy.wait_recv()
    for q in range(8):
        r, c = q // 2 * 8, q % 2 * 128
        grad_ref[r : r + 8, c : c + 128] = done[q]
    for copy in sent + sent_terms + sent_mine + sent_done:
        copy.wait_send()


def tail(part, weight, cotangent):
    vmem = pl.BlockSpec(memory_space=pltpu.VMEM)
    dma = pltpu.SemaphoreType.DMA
    return pl.pallas_call(
        tail_kernel,
        out_shape=(
            jax.ShapeDtypeStruct((256, 256), jnp.bfloat16),
            jax.ShapeDtypeStruct((32, 256), jnp.float32),
        ),
        in_specs=[vmem] * 3,
        out_specs=(vmem, vmem),
        scratch_shapes=[
            pltpu.VMEM((7, 2, 256, TILE), jnp.bfloat16),
            pltpu.VMEM((8, 32, 256), jnp.float32),
            pltpu.VMEM((7, 32, 256), jnp.float32),
            pltpu.VMEM((8, 8, 128), jnp.float32),
            pltpu.VMEM((15, 8, 128), jnp.float32),
            pltpu.VMEM((8, 8, 128), jnp.float32),
            dma((7,)), dma((7,)), dma((7,)), dma((7,)),
            dma((15,)), dma((15,)), dma((7,)), dma((7,)),
        ],
        compiler_params=pltpu.CompilerParams(collective_id=1, has_side_effects=True),
        name="tail",
    )(part, weight, cotangent)


def shards(features, adj_tiles, tile_rows, tile_cols, counts, weight, cotangent):
    sources, slots = adj_tiles.shape[2:4]
    tiles = adj_tiles.reshape(sources * slots, TILE, TILE)
    full = gather(features).reshape(sources, 16, 256, TILE)
    part = aggregate(
        tile_rows.reshape(sources, slots),
        tile_cols.reshape(sources, slots),
        counts.reshape(sources),
        full,
        tiles,
    )
    return tail(part.reshape(8, 2, 256, TILE), weight, cotangent)


def solution(mesh):
    in_specs = (
        P("feat", "blk"),
        P("blk", "feat", None, None, None, None),
        P("blk", "feat", None, None),
        P("blk", "feat", None, None),
        P("blk", "feat", None),
        P(),
        P(None, ("blk", "feat")),
    )
    out_specs = (P(None, ("blk", "feat")), P("feat", None))
    return jax.shard_map(shards, mesh=mesh, in_specs=in_specs, out_specs=out_specs, check_vma=False)
```

```python
import functools
import math

import jax
import jax.numpy as jnp
from jax import lax
from jax.experimental import pallas as pl
from jax.experimental.pallas import tpu as pltpu
from jax.sharding import PartitionSpec as P

MESH = pl.DeviceIdType.MESH
TILE = 128
ORDERS = (("x", "y", "z"), ("y", "z", "x"), ("z", "x", "y"))
COLUMNS = ((0, 6), (6, 11), (11, 16))
MIB = 2**20


EARLY = 24


def in_vmem(array):
    return pltpu.with_memory_space_constraint(array, pltpu.VMEM)


def in_hbm(array):
    return pltpu.with_memory_space_constraint(array, pltpu.HBM)


def place():
    blk = lax.axis_index("blk")
    feat = lax.axis_index("feat")
    return {
        "x": (feat % 2) * 2 + blk // 8,
        "y": (blk // 2) % 4,
        "z": feat // 2,
        "c": blk % 2,
    }


def device(at):
    return {
        "blk": ((at["x"] % 2) * 4 + at["y"]) * 2 + at["c"],
        "feat": at["z"] * 2 + at["x"] // 2,
    }


def moved(at, dim, by):
    return {**at, dim: (at[dim] + by) % (2 if dim == "c" else 4)}


class Sender:
    def __init__(self, send_sem, recv_sem):
        self.send_sem, self.recv_sem, self.used, self.all = send_sem, recv_sem, 0, []

    def start(self, ref, to):
        i = self.used
        self.used += 1
        copy = pltpu.make_async_remote_copy(
            src_ref=ref,
            dst_ref=ref,
            send_sem=self.send_sem.at[i],
            recv_sem=self.recv_sem.at[i],
            device_id=device(to),
            device_id_type=MESH,
        )
        self.all.append(copy)
        copy.start()
        return copy


N_COPIES = 3 * 50


class Ring:
    def __init__(self, net, me, order, span, full):
        self.net, self.me, self.order, self.span, self.full = net, me, order, span, full
        self.first, self.size = span[0] * 128, span[1] - span[0]
        self.p1, self.p2, self.p3 = (me[d] for d in order)
        self.went, self.passed = {}, []

    def place(self, by1, by2, by3):
        at = (self.me["c"] * 4 + (self.p3 + by3) % 4) * 4 + (self.p2 + by2) % 4
        return self.first + (at * 4 + by1) * self.size

    def block(self, by1, by2=0, by3=0):
        return self.full.at[pl.ds(self.place((self.p1 + by1) % 4, by2, by3), self.size)]

    def line(self, by3, by2):
        return self.full.at[pl.ds(self.place(0, by2, by3), 4 * self.size)]

    def spread(self, by1):
        for name, by in (("p", 1), ("m", 3)):
            self.send(f"{name}{by1}", self.block(by1), 2, by)
        for name, by in (("u0", 1), ("v0", 3)):
            self.send(f"{name}{by1}", self.block(by1), 3, by)

    def out(self, by2):
        self.send(f"u{by2}", self.line(0, by2), 3, 1)
        self.send(f"v{by2}", self.line(0, by2), 3, 3)
        self.share(self.line(0, by2))

    def send(self, name, ref, step, by):
        to = moved(self.me, self.order[step - 1], by)
        self.went[name] = self.net.start(ref, to)

    def came(self, *names):
        for name in names:
            self.went[name].wait_recv()

    def share(self, ref):
        self.passed.append(self.net.start(ref, moved(self.me, "c", 1)))


def gather_kernel(
    x_ref, tiles_hbm, rows_hbm, cols_hbm, full, tiles, codes,
    rows, cols, own_sem, slot_sem, tile_sem, send_sem, recv_sem,
):
    me = place()
    sibling = moved(me, "c", 1)
    neighbours = [moved(me, d, by) for d in "xyz" for by in (1, 3)] + [sibling]
    barrier = pltpu.get_barrier_semaphore()
    for other in neighbours:
        pl.semaphore_signal(barrier, inc=1, device_id=device(other), device_id_type=MESH)
    slot_loads = [
        pltpu.make_async_copy(rows_hbm, rows, slot_sem.at[0]),
        pltpu.make_async_copy(cols_hbm, cols, slot_sem.at[1]),
    ]
    for copy in slot_loads:
        copy.start()
    net = Sender(send_sem, recv_sem)
    rings = [
        Ring(net, me, order, span, full)
        for order, span in zip(ORDERS, COLUMNS)
    ]
    own = []
    for r in rings:
        for i, ct in enumerate(range(*r.span)):
            own.append(
                pltpu.make_async_copy(
                    x_ref.at[:, ct * TILE : (ct + 1) * TILE],
                    r.full.at[r.place(r.p1, 0, 0) + i],
                    own_sem.at[ct],
                )
            )
            own[-1].start()
    for copy in own:
        copy.wait()
    pl.semaphore_wait(barrier, len(neighbours))

    lower, upper = (slice(None), slice(0, 16)), (slice(None), slice(16, 32))
    for r in rings:
        r.send("a", r.block(0), 1, 1)
        r.send("b", r.block(0), 1, 3)
    for r in rings:
        r.spread(0)
    sources = rows.shape[0]
    slots = tiles_hbm.shape[0] // sources
    loads = []
    for i in range(sources):
        copy = pltpu.make_async_copy(
            tiles_hbm.at[i * slots : i * slots + EARLY],
            tiles.at[i * EARLY : (i + 1) * EARLY],
            tile_sem.at[i],
        )
        loads.append(copy)
        loads[-1].start()
    for copy in slot_loads:
        copy.wait()
    codes[...] = slot_codes(rows[...], cols[...])
    for r in rings:
        r.came("a")
        r.send("af", r.block(3).at[lower], 1, 1)
        r.came("b")
        r.send("bf", r.block(1).at[upper], 1, 3)
    for r in rings:
        r.spread(3)
        r.spread(1)
    for r in rings:
        r.came("p0")
        r.send("pf0", r.block(0, 3), 2, 1)
    for r in rings:
        r.came("af", "bf")
        r.spread(2)
        r.share(r.line(0, 0))
    for r in rings:
        r.came("p3")
        r.send("pf3", r.block(3, 3), 2, 1)
        r.came("m1")
        r.send("mf1", r.block(1, 1), 2, 3)
    for r in rings:
        r.came("m0", "m3", "m2")
        r.send("mf2", r.block(2, 1), 2, 3)
        r.out(1)
        r.came("p1", "p2")
        r.out(3)
    for r in rings:
        r.came("u00", "u03", "u01", "u02")
        r.send("u0f", r.line(3, 0), 3, 1)
        r.share(r.line(3, 0))
        r.came("v00", "v03", "v01", "v02")
        r.share(r.line(1, 0))
    for r in rings:
        r.came("pf0", "pf3", "mf1", "mf2")
        r.out(2)
    for name, by3, by2, on in (
        ("v1", 1, 1, 3), ("u3", 3, 3, 1), ("u1", 3, 1, 0), ("v3", 1, 3, 0),
        ("v2", 1, 2, 3), ("u2", 3, 2, 0),
    ):
        for r in rings:
            r.came(name)
            if on:
                r.send(name + "f", r.line(by3, by2), 3, on)
            r.share(r.line(by3, by2))
    for name, by2 in (("u0f", 0), ("u3f", 3), ("v1f", 1), ("v2f", 2)):
        for r in rings:
            r.came(name)
            r.share(r.line(2, by2))
    for r in rings:
        for copy in r.passed:
            copy.wait_recv()
    for copy in net.all:
        copy.wait_send()
    for copy in loads:
        copy.wait()


def slot_codes(rows, cols):
    source = lax.broadcasted_iota(jnp.int32, rows.shape, 0)
    slot = lax.broadcasted_iota(jnp.int32, rows.shape, 1)
    c, y, x = source & 1, (source >> 1) & 3, source >> 3
    at = {"c": c, "x": x, "y": y, "z": jnp.zeros_like(x)}
    block, order = 0, 0
    for i, (dims, (lo, hi)) in enumerate(zip(ORDERS, COLUMNS)):
        d1, d2, d3 = (at[d] for d in dims)
        here = lo * 128 + (((c * 4 + d3) * 4 + d2) * 4 + d1) * (hi - lo) + cols - lo
        block, order = jnp.where(cols >= lo, here, block), jnp.where(cols >= lo, i, order)
    tile = source * EARLY + jnp.where(slot < EARLY, slot, slot - EARLY)
    return (tile << 18) | (block << 7) | (order << 5) | rows


def strides(dim):
    return [(hi - lo) * 4 ** dims.index(dim) for dims, (lo, hi) in zip(ORDERS, COLUMNS)]


def gather(features, tiles, rows, cols):
    hbm = pl.BlockSpec(memory_space=pltpu.HBM)
    vmem = pl.BlockSpec(memory_space=pltpu.VMEM)
    dma = pltpu.SemaphoreType.DMA
    return pl.pallas_call(
        gather_kernel,
        out_shape=(
            pltpu.VMEM((2048, 32, TILE), jnp.bfloat16),
            pltpu.VMEM((tiles.shape[0] // 2, TILE, TILE), jnp.bfloat16),
            jax.ShapeDtypeStruct(rows.shape, jnp.int32),
        ),
        in_specs=[hbm] * 4,
        out_specs=(vmem, vmem, vmem),
        scratch_shapes=[
            pltpu.VMEM(rows.shape, jnp.int32), pltpu.VMEM(cols.shape, jnp.int32),
            dma((16,)), dma((2,)), dma((rows.shape[0],)), dma((N_COPIES,)), dma((N_COPIES,)),
        ],
        compiler_params=pltpu.CompilerParams(
            collective_id=0, has_side_effects=True, vmem_limit_bytes=2 * MIB
        ),
        name="gather",
    )(*(in_hbm(a) for a in (features, tiles, rows, cols)))


BATCH = 32


def aggregate_kernel(
    codes, counts, full, early, tiles_hbm, out_ref, late, total, listed, late_sem
):
    sources, slots = codes.shape

    def late_copy(s):
        return pltpu.make_async_copy(
            tiles_hbm.at[pl.ds(s * slots + EARLY, EARLY)],
            late.at[pl.ds(s * EARLY, EARLY)],
            late_sem.at[s],
        )

    @pl.loop(0, sources)
    def _(s):
        pl.when(counts[s] > EARLY)(lambda: late_copy(s).start())

    total[...] = jnp.zeros_like(total)

    def enlist(first):
        def enter(s, end):
            live = jnp.clip(counts[s] - first, 0, EARLY)

            def eight(j, carry):
                for u in range(8):
                    listed[end + j * 8 + u] = codes[s, first + j * 8 + u]
                return carry

            lax.fori_loop(0, (live + 7) >> 3, eight, 0)
            return end + live

        end = lax.fori_loop(0, sources, enter, 0)
        for u in range(BATCH):
            listed[end + u] = out_ref.shape[0]
        return (end + BATCH - 1) // BATCH

    def pick(order, values):
        return jnp.where(order == 0, values[0], jnp.where(order == 1, values[1], values[2]))

    def panel(code):
        block, order = (code >> 7) & 2047, (code >> 5) & 3
        step_z, step_x = pick(order, strides("z")), pick(order, strides("x")) * 2
        parts = [full[block + z * step_z + x_hi * step_x] for z in range(4) for x_hi in range(2)]
        return jnp.concatenate(parts, axis=0)

    def work(steps, tiles):
        @pl.loop(0, steps)
        def _(b):
            for part in range(0, BATCH, BATCH // 2):
                entries = [listed[b * BATCH + part + u] for u in range(BATCH // 2)]
                products = [
                    lax.dot_general(
                        panel(code),
                        tiles[code >> 18],
                        (((1,), (1,)), ((), ())),
                        preferred_element_type=jnp.float32,
                    )
                    for code in entries
                ]
                for code, product in zip(entries, products):
                    total[code & 31] += product

    work(enlist(0), early)

    @pl.loop(0, sources)
    def _(s):
        pl.when(counts[s] > EARLY)(lambda: late_copy(s).wait())

    work(enlist(EARLY), late)
    out_ref[...] = total[: out_ref.shape[0]].astype(out_ref.dtype)


def aggregate(codes, counts, full, early, tiles):
    smem = pl.BlockSpec(memory_space=pltpu.SMEM)
    vmem = pl.BlockSpec(memory_space=pltpu.VMEM)
    return pl.pallas_call(
        aggregate_kernel,
        out_shape=pltpu.VMEM((16, 256, TILE), jnp.bfloat16),
        in_specs=[smem, smem, vmem, vmem, pl.BlockSpec(memory_space=pltpu.HBM)],
        out_specs=vmem,
        scratch_shapes=[
            pltpu.VMEM(early.shape, jnp.bfloat16),
            pltpu.VMEM((17, 256, TILE), jnp.float32),
            pltpu.SMEM((codes.size // 2 + BATCH + 8,), jnp.int32),
            pltpu.SemaphoreType.DMA((codes.shape[0],)),
        ],
        compiler_params=pltpu.CompilerParams(vmem_limit_bytes=17 * MIB),
        name="aggregate",
    )(codes, counts, in_vmem(full), in_vmem(early), in_hbm(tiles))


def tail_kernel(
    part, weight, cotangent, act_ref, sums_ref,
    held, terms, terms_in, psem, pin, tsem, tin, msem, min_,
):
    blk, feat = lax.axis_index("blk"), lax.axis_index("feat")
    barrier = pltpu.get_barrier_semaphore()
    for i in range(1, 8):
        pl.semaphore_signal(
            barrier, inc=1, device_id={"feat": (feat + i) % 8}, device_id_type=MESH
        )
    for i in range(1, 16):
        pl.semaphore_signal(
            barrier, inc=1, device_id={"blk": (blk + i) % 16}, device_id_type=MESH
        )
    pl.semaphore_wait(barrier, 22)

    def remote(src, dst, send, recv, to):
        copy = pltpu.make_async_remote_copy(
            src_ref=src, dst_ref=dst, send_sem=send, recv_sem=recv,
            device_id=to, device_id_type=MESH,
        )
        copy.start()
        return copy

    sent = []
    for i in range(1, 8):
        to = (feat + i) % 8
        sent.append(
            remote(part.at[to], held.at[i - 1], psem.at[i - 1], pin.at[i - 1], {"feat": to})
        )
    summed = part[feat].astype(jnp.float32)
    for i in range(7):
        sent[i].wait_recv()
        summed = summed + held[i].astype(jnp.float32)
    nodes = summed.astype(jnp.bfloat16)
    nodes = jnp.concatenate([nodes[0], nodes[1]], axis=1)
    preact = jnp.dot(weight[...], nodes, preferred_element_type=jnp.float32)
    sigmoid = jax.nn.sigmoid(preact)
    act_ref[...] = (preact * sigmoid).astype(jnp.bfloat16)
    slope = cotangent[...].astype(jnp.float32) * sigmoid * (1.0 + preact * (1.0 - sigmoid))
    local = lax.dot_general(
        slope.astype(jnp.bfloat16),
        nodes,
        (((1,), (1,)), ((), ())),
        preferred_element_type=jnp.float32,
    )
    terms[...] = local.reshape(terms.shape)
    sent_terms = []
    for i in range(1, 8):
        to = (feat + i) % 8
        sent_terms.append(
            remote(terms.at[to], terms_in.at[i - 1], tsem.at[i - 1], tin.at[i - 1], {"feat": to})
        )
    share = terms[feat]
    for i in range(7):
        sent_terms[i].wait_recv()
        share = share + terms_in[i]
    sums_ref[blk] = share.astype(sums_ref.dtype)
    sent_sums = []
    for i in range(1, 16):
        sent_sums.append(
            remote(
                sums_ref.at[blk], sums_ref.at[blk], msem.at[i - 1], min_.at[i - 1],
                {"blk": (blk + i) % 16},
            )
        )
    for copy in sent_sums:
        copy.wait_recv()
    for copy in sent + sent_terms + sent_sums:
        copy.wait_send()


def tail(part, weight, cotangent):
    vmem = pl.BlockSpec(memory_space=pltpu.VMEM)
    dma = pltpu.SemaphoreType.DMA
    return pl.pallas_call(
        tail_kernel,
        out_shape=(
            pltpu.VMEM((256, 256), jnp.bfloat16),
            pltpu.VMEM((16, 32, 256), jnp.bfloat16),
        ),
        in_specs=[vmem] * 3,
        out_specs=(vmem, vmem),
        scratch_shapes=[
            pltpu.VMEM((7, 2, 256, TILE), jnp.bfloat16),
            pltpu.VMEM((8, 32, 256), jnp.float32),
            pltpu.VMEM((7, 32, 256), jnp.float32),
            dma((7,)), dma((7,)), dma((7,)), dma((7,)), dma((15,)), dma((15,)),
        ],
        compiler_params=pltpu.CompilerParams(collective_id=1, has_side_effects=True),
        name="tail",
    )(in_vmem(part), weight, cotangent)


def finish_kernel(act, sums, act_ref, grad_ref):
    act_ref[...] = act[...]
    grad_ref[...] = jnp.sum(sums[...].astype(jnp.float32), axis=0) * (1.0 / math.sqrt(32768))


def finish(act, sums):
    vmem = pl.BlockSpec(memory_space=pltpu.VMEM)
    return pl.pallas_call(
        finish_kernel,
        out_shape=(
            jax.ShapeDtypeStruct(act.shape, act.dtype),
            jax.ShapeDtypeStruct(sums.shape[1:], jnp.float32),
        ),
        in_specs=[vmem] * 2,
        out_specs=(vmem, vmem),
        name="finish",
    )(in_vmem(act), in_vmem(sums))


def shards(features, adj_tiles, tile_rows, tile_cols, counts, weight, cotangent):
    sources, slots = adj_tiles.shape[2:4]
    tiles = adj_tiles.reshape(sources * slots, TILE, TILE)
    rows, cols = (a.reshape(sources, slots) for a in (tile_rows, tile_cols))
    full, early, codes = gather(features, tiles, rows, cols)
    part = aggregate(codes, counts.reshape(sources), full, early, tiles)
    part = part.reshape(8, 2, 256, TILE)
    return finish(*tail(part, weight, cotangent))


def solution(mesh):
    in_specs = (
        P("feat", "blk"),
        P("blk", "feat", None, None, None, None),
        P("blk", "feat", None, None),
        P("blk", "feat", None, None),
        P("blk", "feat", None),
        P(),
        P(None, ("blk", "feat")),
    )
    out_specs = (P(None, ("blk", "feat")), P("feat", None))
    return jax.shard_map(shards, mesh=mesh, in_specs=in_specs, out_specs=out_specs, check_vma=False)
```

```python
import functools
import math

import jax
import jax.numpy as jnp
from jax import lax
from jax.experimental import pallas as pl
from jax.experimental.pallas import tpu as pltpu
from jax.sharding import PartitionSpec as P

MESH = pl.DeviceIdType.MESH
TILE = 128
ORDERS = (("x", "y", "z"), ("y", "z", "x"), ("z", "x", "y"))
COLUMNS = (((0, 6), (6, 11), (11, 16)), ((0, 5), (5, 11), (11, 16)))
MIB = 2**20


EARLY = 24


def in_vmem(array):
    return pltpu.with_memory_space_constraint(array, pltpu.VMEM)


def in_hbm(array):
    return pltpu.with_memory_space_constraint(array, pltpu.HBM)


def place():
    blk = lax.axis_index("blk")
    feat = lax.axis_index("feat")
    return {
        "x": (feat % 2) * 2 + blk // 8,
        "y": (blk // 2) % 4,
        "z": feat // 2,
        "c": blk % 2,
    }


def device(at):
    return {
        "blk": ((at["x"] % 2) * 4 + at["y"]) * 2 + at["c"],
        "feat": at["z"] * 2 + at["x"] // 2,
    }


def moved(at, dim, by):
    return {**at, dim: (at[dim] + by) % (2 if dim == "c" else 4)}


class Sender:
    def __init__(self, send_sem, recv_sem):
        self.send_sem, self.recv_sem, self.used, self.all = send_sem, recv_sem, 0, []

    def start(self, ref, to, comes=None):
        i = self.used
        self.used += 1

        def copy_of(ref):
            return pltpu.make_async_remote_copy(
                src_ref=ref,
                dst_ref=ref,
                send_sem=self.send_sem.at[i],
                recv_sem=self.recv_sem.at[i],
                device_id=device(to),
                device_id_type=MESH,
            )

        copy = copy_of(ref)
        self.all.append(copy)
        copy.start()
        return copy if comes is None else copy_of(comes)


N_COPIES = 3 * 50


def first_block(core, span):
    return core * 1024 + span[0] * 64


class Ring:
    def __init__(self, net, me, core, which, full):
        self.net, self.me, self.core, self.which, self.full = net, me, core, which, full
        self.order, self.span = ORDERS[which], COLUMNS[core][which]
        self.size = self.span[1] - self.span[0]
        self.p1, self.p2, self.p3 = (me[d] for d in self.order)
        self.went, self.passed = {}, []

    def place(self, by1, by2, by3):
        at = ((self.p3 + by3) % 4 * 4 + (self.p2 + by2) % 4) * 4 + by1
        return first_block(self.core, self.span) + at * self.size

    def block(self, by1, by2=0, by3=0):
        return self.full.at[pl.ds(self.place((self.p1 + by1) % 4, by2, by3), self.size)]

    def line(self, by3, by2):
        return self.full.at[pl.ds(self.place(0, by2, by3), 4 * self.size)]

    def spread(self, by1):
        for name, by in (("p", 1), ("m", 3)):
            self.send(f"{name}{by1}", self.block(by1), 2, by)
        for name, by in (("u0", 1), ("v0", 3)):
            self.send(f"{name}{by1}", self.block(by1), 3, by)

    def out(self, by2, *bys):
        for by in bys:
            self.send(f"{'u' if by == 1 else 'v'}{by2}", self.line(0, by2), 3, by)

    def send(self, name, ref, step, by):
        to = moved(self.me, self.order[step - 1], by)
        self.went[name] = self.net.start(ref, to)

    def came(self, *names):
        for name in names:
            self.went[name].wait_recv()

    def share(self, by3, by2):
        to = moved(self.me, "c", 1)
        theirs = Ring(self.net, self.me, 1 - self.core, self.which, self.full)
        self.passed.append(self.net.start(self.line(by3, by2), to, theirs.line(by3, by2)))


def gather_kernel(
    x_ref, tiles_hbm, rows_hbm, cols_hbm, full, tiles, codes,
    rows, cols, own_sem, slot_sem, tile_sem, send_sem, recv_sem,
):
    me = place()
    sibling = moved(me, "c", 1)
    neighbours = [moved(me, d, by) for d in "xyz" for by in (1, 3)] + [sibling]
    barrier = pltpu.get_barrier_semaphore()
    for other in neighbours:
        pl.semaphore_signal(barrier, inc=1, device_id=device(other), device_id_type=MESH)
    slot_loads = [
        pltpu.make_async_copy(rows_hbm, rows, slot_sem.at[0]),
        pltpu.make_async_copy(cols_hbm, cols, slot_sem.at[1]),
    ]
    for copy in slot_loads:
        copy.start()
    for core in range(2):
        pl.when(me["c"] == core)(
            functools.partial(
                gather_core, core, me, neighbours, barrier, x_ref, tiles_hbm, full, tiles, codes,
                rows, cols, slot_loads, own_sem, tile_sem, send_sem, recv_sem,
            )
        )


def gather_core(
    core, me, neighbours, barrier, x_ref, tiles_hbm, full, tiles, codes,
    rows, cols, slot_loads, own_sem, tile_sem, send_sem, recv_sem,
):
    net = Sender(send_sem, recv_sem)
    rings = [Ring(net, me, core, which, full) for which in range(3)]
    own = []
    for r in rings:
        for i, ct in enumerate(range(*r.span)):
            own.append(
                pltpu.make_async_copy(
                    x_ref.at[:, ct * TILE : (ct + 1) * TILE],
                    r.full.at[r.place(r.p1, 0, 0) + i],
                    own_sem.at[ct],
                )
            )
            own[-1].start()
    for copy in own:
        copy.wait()
    pl.semaphore_wait(barrier, len(neighbours))

    lower, upper = (slice(None), slice(0, 16)), (slice(None), slice(16, 32))
    for r in rings:
        r.send("a", r.block(0), 1, 1)
        r.send("b", r.block(0), 1, 3)
    for r in rings:
        r.spread(0)
    sources = rows.shape[0]
    slots = tiles_hbm.shape[0] // sources
    loads = []
    for i in range(sources):
        copy = pltpu.make_async_copy(
            tiles_hbm.at[i * slots : i * slots + EARLY],
            tiles.at[i * EARLY : (i + 1) * EARLY],
            tile_sem.at[i],
        )
        loads.append(copy)
        loads[-1].start()
    for copy in slot_loads:
        copy.wait()
    codes[...] = slot_codes(rows[...], cols[...])
    for r in rings:
        r.came("a")
        r.send("af", r.block(3).at[lower], 1, 1)
        r.came("b")
        r.send("bf", r.block(1).at[upper], 1, 3)
    for r in rings:
        r.spread(3)
        r.spread(1)
    for r in rings:
        r.came("p0")
        r.send("pf0", r.block(0, 3), 2, 1)
    for r in rings:
        r.came("af", "bf")
        r.spread(2)
        r.share(0, 0)
    for r in rings:
        r.came("p3")
        r.send("pf3", r.block(3, 3), 2, 1)
        r.came("m1")
        r.send("mf1", r.block(1, 1), 2, 3)
    for r in rings:
        r.came("m0", "m3", "m2")
        r.send("mf2", r.block(2, 1), 2, 3)
        r.out(1, 3)
        r.came("p1", "p2")
        r.out(3, 1, 3)
        r.out(1, 1)
        r.share(0, 1)
        r.share(0, 3)
    for r in rings:
        r.came("u00", "u03", "u01", "u02")
        r.send("u0f", r.line(3, 0), 3, 1)
        r.share(3, 0)
        r.came("v00", "v03", "v01", "v02")
        r.share(1, 0)
    for r in rings:
        r.came("pf0", "pf3", "mf1", "mf2")
        r.out(2, 3, 1)
        r.share(0, 2)
    for name, by3, by2, on in (
        ("v1", 1, 1, 3), ("u3", 3, 3, 1), ("u1", 3, 1, 0), ("v3", 1, 3, 0),
        ("v2", 1, 2, 3), ("u2", 3, 2, 0),
    ):
        for r in rings:
            r.came(name)
            if on:
                r.send(name + "f", r.line(by3, by2), 3, on)
            r.share(by3, by2)
    for name, by2 in (("u0f", 0), ("u3f", 3), ("v1f", 1), ("v2f", 2)):
        for r in rings:
            r.came(name)
            r.share(2, by2)
    for r in rings:
        for copy in r.passed:
            copy.wait_recv()
    for copy in net.all:
        copy.wait_send()
    for copy in loads:
        copy.wait()


def slot_codes(rows, cols):
    source = lax.broadcasted_iota(jnp.int32, rows.shape, 0)
    slot = lax.broadcasted_iota(jnp.int32, rows.shape, 1)
    c, y, x = source & 1, (source >> 1) & 3, source >> 3
    at = {"x": x, "y": y, "z": jnp.zeros_like(x)}
    block, layout = 0, 0
    for core in range(2):
        for i, (dims, span) in enumerate(zip(ORDERS, COLUMNS[core])):
            d1, d2, d3 = (at[d] for d in dims)
            size = span[1] - span[0]
            here = first_block(core, span) + ((d3 * 4 + d2) * 4 + d1) * size + cols - span[0]
            inside = (c == core) & (cols >= span[0])
            block = jnp.where(inside, here, block)
            layout = jnp.where(inside, core * 3 + i, layout)
    tile = source * EARLY + jnp.where(slot < EARLY, slot, slot - EARLY)
    return (tile << 19) | (block << 8) | (layout << 5) | rows


def strides(dim):
    return [
        (hi - lo) * 4 ** dims.index(dim)
        for columns in COLUMNS
        for dims, (lo, hi) in zip(ORDERS, columns)
    ]


def gather(features, tiles, rows, cols):
    hbm = pl.BlockSpec(memory_space=pltpu.HBM)
    vmem = pl.BlockSpec(memory_space=pltpu.VMEM)
    dma = pltpu.SemaphoreType.DMA
    return pl.pallas_call(
        gather_kernel,
        out_shape=(
            pltpu.VMEM((2048, 32, TILE), jnp.bfloat16),
            pltpu.VMEM((tiles.shape[0] // 2, TILE, TILE), jnp.bfloat16),
            jax.ShapeDtypeStruct(rows.shape, jnp.int32),
        ),
        in_specs=[hbm] * 4,
        out_specs=(vmem, vmem, vmem),
        scratch_shapes=[
            pltpu.VMEM(rows.shape, jnp.int32), pltpu.VMEM(cols.shape, jnp.int32),
            dma((16,)), dma((2,)), dma((rows.shape[0],)), dma((N_COPIES,)), dma((N_COPIES,)),
        ],
        compiler_params=pltpu.CompilerParams(
            collective_id=0, has_side_effects=True, vmem_limit_bytes=2 * MIB
        ),
        name="gather",
    )(*(in_hbm(a) for a in (features, tiles, rows, cols)))


BATCH = 32


def aggregate_kernel(
    codes, counts, full, early, tiles_hbm, out_ref,
    late, total, listed, steps_z, steps_x, late_sem,
):
    sources, slots = codes.shape

    def late_copy(s):
        return pltpu.make_async_copy(
            tiles_hbm.at[pl.ds(s * slots + EARLY, EARLY)],
            late.at[pl.ds(s * EARLY, EARLY)],
            late_sem.at[s],
        )

    @pl.loop(0, sources)
    def _(s):
        pl.when(counts[s] > EARLY)(lambda: late_copy(s).start())

    total[...] = jnp.zeros_like(total)

    def enlist(first):
        def enter(s, end):
            live = jnp.clip(counts[s] - first, 0, EARLY)

            def eight(j, carry):
                for u in range(8):
                    listed[end + j * 8 + u] = codes[s, first + j * 8 + u]
                return carry

            lax.fori_loop(0, (live + 7) >> 3, eight, 0)
            return end + live

        end = lax.fori_loop(0, sources, enter, 0)
        for u in range(BATCH):
            listed[end + u] = out_ref.shape[0]
        return (end + BATCH - 1) // BATCH

    for i in range(6):
        steps_z[i] = strides("z")[i]
        steps_x[i] = strides("x")[i] * 2

    def panel(code):
        block, layout = (code >> 8) & 2047, (code >> 5) & 7
        step_z, step_x = steps_z[layout], steps_x[layout]
        parts = [full[block + z * step_z + x_hi * step_x] for z in range(4) for x_hi in range(2)]
        return jnp.concatenate(parts, axis=0)

    def work(steps, tiles):
        @pl.loop(0, steps)
        def _(b):
            for part in range(0, BATCH, BATCH // 2):
                entries = [listed[b * BATCH + part + u] for u in range(BATCH // 2)]
                products = [
                    lax.dot_general(
                        panel(code),
                        tiles[code >> 19],
                        (((1,), (1,)), ((), ())),
                        preferred_element_type=jnp.float32,
                    )
                    for code in entries
                ]
                for code, product in zip(entries, products):
                    total[code & 31] += product

    work(enlist(0), early)

    @pl.loop(0, sources)
    def _(s):
        pl.when(counts[s] > EARLY)(lambda: late_copy(s).wait())

    work(enlist(EARLY), late)
    out_ref[...] = total[: out_ref.shape[0]].astype(out_ref.dtype)


def aggregate(codes, counts, full, early, tiles):
    smem = pl.BlockSpec(memory_space=pltpu.SMEM)
    vmem = pl.BlockSpec(memory_space=pltpu.VMEM)
    return pl.pallas_call(
        aggregate_kernel,
        out_shape=pltpu.VMEM((16, 256, TILE), jnp.bfloat16),
        in_specs=[smem, smem, vmem, vmem, pl.BlockSpec(memory_space=pltpu.HBM)],
        out_specs=vmem,
        scratch_shapes=[
            pltpu.VMEM(early.shape, jnp.bfloat16),
            pltpu.VMEM((17, 256, TILE), jnp.float32),
            pltpu.SMEM((codes.size // 2 + BATCH + 8,), jnp.int32),
            pltpu.SMEM((6,), jnp.int32),
            pltpu.SMEM((6,), jnp.int32),
            pltpu.SemaphoreType.DMA((codes.shape[0],)),
        ],
        compiler_params=pltpu.CompilerParams(vmem_limit_bytes=17 * MIB),
        name="aggregate",
    )(codes, counts, in_vmem(full), in_vmem(early), in_hbm(tiles))


def tail_kernel(
    part, weight, cotangent, act_ref, sums_ref,
    held, terms, terms_in, psem, pin, tsem, tin, msem, min_,
):
    blk, feat = lax.axis_index("blk"), lax.axis_index("feat")
    barrier = pltpu.get_barrier_semaphore()
    for i in range(1, 8):
        pl.semaphore_signal(
            barrier, inc=1, device_id={"feat": (feat + i) % 8}, device_id_type=MESH
        )
    for i in range(1, 16):
        pl.semaphore_signal(
            barrier, inc=1, device_id={"blk": (blk + i) % 16}, device_id_type=MESH
        )
    pl.semaphore_wait(barrier, 22)

    def remote(src, dst, send, recv, to):
        copy = pltpu.make_async_remote_copy(
            src_ref=src, dst_ref=dst, send_sem=send, recv_sem=recv,
            device_id=to, device_id_type=MESH,
        )
        copy.start()
        return copy

    sent = []
    for i in range(1, 8):
        to = (feat + i) % 8
        sent.append(
            remote(part.at[to], held.at[i - 1], psem.at[i - 1], pin.at[i - 1], {"feat": to})
        )
    summed = part[feat].astype(jnp.float32)
    for i in range(7):
        sent[i].wait_recv()
        summed = summed + held[i].astype(jnp.float32)
    nodes = summed.astype(jnp.bfloat16)
    nodes = jnp.concatenate([nodes[0], nodes[1]], axis=1)
    preact = jnp.dot(weight[...], nodes, preferred_element_type=jnp.float32)
    sigmoid = jax.nn.sigmoid(preact)
    act_ref[...] = (preact * sigmoid).astype(jnp.bfloat16)
    slope = cotangent[...].astype(jnp.float32) * sigmoid * (1.0 + preact * (1.0 - sigmoid))
    local = lax.dot_general(
        slope.astype(jnp.bfloat16),
        nodes,
        (((1,), (1,)), ((), ())),
        preferred_element_type=jnp.float32,
    )
    terms[...] = local.reshape(terms.shape).astype(terms.dtype)
    sent_terms = []
    for i in range(1, 8):
        to = (feat + i) % 8
        sent_terms.append(
            remote(terms.at[to], terms_in.at[i - 1], tsem.at[i - 1], tin.at[i - 1], {"feat": to})
        )
    share = terms[feat].astype(jnp.float32)
    for i in range(7):
        sent_terms[i].wait_recv()
        share = share + terms_in[i].astype(jnp.float32)
    sums_ref[blk] = share.astype(sums_ref.dtype)
    sent_sums = []
    for i in range(1, 16):
        sent_sums.append(
            remote(
                sums_ref.at[blk], sums_ref.at[blk], msem.at[i - 1], min_.at[i - 1],
                {"blk": (blk + i) % 16},
            )
        )
    for copy in sent_sums:
        copy.wait_recv()
    for copy in sent + sent_terms + sent_sums:
        copy.wait_send()


def tail(part, weight, cotangent):
    vmem = pl.BlockSpec(memory_space=pltpu.VMEM)
    dma = pltpu.SemaphoreType.DMA
    return pl.pallas_call(
        tail_kernel,
        out_shape=(
            pltpu.VMEM((256, 256), jnp.bfloat16),
            pltpu.VMEM((16, 32, 256), jnp.bfloat16),
        ),
        in_specs=[vmem] * 3,
        out_specs=(vmem, vmem),
        scratch_shapes=[
            pltpu.VMEM((7, 2, 256, TILE), jnp.bfloat16),
            pltpu.VMEM((8, 32, 256), jnp.bfloat16),
            pltpu.VMEM((7, 32, 256), jnp.bfloat16),
            dma((7,)), dma((7,)), dma((7,)), dma((7,)), dma((15,)), dma((15,)),
        ],
        compiler_params=pltpu.CompilerParams(collective_id=1, has_side_effects=True),
        name="tail",
    )(in_vmem(part), weight, cotangent)


def finish_kernel(act, sums, act_ref, grad_ref):
    act_ref[...] = act[...]
    grad_ref[...] = jnp.sum(sums[...].astype(jnp.float32), axis=0) * (1.0 / math.sqrt(32768))


def finish(act, sums):
    vmem = pl.BlockSpec(memory_space=pltpu.VMEM)
    return pl.pallas_call(
        finish_kernel,
        out_shape=(
            jax.ShapeDtypeStruct(act.shape, act.dtype),
            jax.ShapeDtypeStruct(sums.shape[1:], jnp.float32),
        ),
        in_specs=[vmem] * 2,
        out_specs=(vmem, vmem),
        name="finish",
    )(in_vmem(act), in_vmem(sums))


def shards(features, adj_tiles, tile_rows, tile_cols, counts, weight, cotangent):
    sources, slots = adj_tiles.shape[2:4]
    tiles = adj_tiles.reshape(sources * slots, TILE, TILE)
    rows, cols = (a.reshape(sources, slots) for a in (tile_rows, tile_cols))
    full, early, codes = gather(features, tiles, rows, cols)
    part = aggregate(codes, counts.reshape(sources), full, early, tiles)
    part = part.reshape(8, 2, 256, TILE)
    return finish(*tail(part, weight, cotangent))


def solution(mesh):
    in_specs = (
        P("feat", "blk"),
        P("blk", "feat", None, None, None, None),
        P("blk", "feat", None, None),
        P("blk", "feat", None, None),
        P("blk", "feat", None),
        P(),
        P(None, ("blk", "feat")),
    )
    out_specs = (P(None, ("blk", "feat")), P("feat", None))
    return jax.shard_map(shards, mesh=mesh, in_specs=in_specs, out_specs=out_specs, check_vma=False)
```

```python
import functools
import math

import jax
import jax.numpy as jnp
from jax import lax
from jax.experimental import pallas as pl
from jax.experimental.pallas import tpu as pltpu
from jax.sharding import PartitionSpec as P

MESH = pl.DeviceIdType.MESH
TILE = 128
ORDERS = (("x", "y", "z"), ("y", "z", "x"), ("z", "x", "y"))
COLUMNS = (((0, 6), (6, 11), (11, 16)), ((0, 5), (5, 11), (11, 16)))
MIB = 2**20


EARLY = 24


def in_vmem(array):
    return pltpu.with_memory_space_constraint(array, pltpu.VMEM)


def in_hbm(array):
    return pltpu.with_memory_space_constraint(array, pltpu.HBM)


def place():
    blk = lax.axis_index("blk")
    feat = lax.axis_index("feat")
    return {
        "x": (feat % 2) * 2 + blk // 8,
        "y": (blk // 2) % 4,
        "z": feat // 2,
        "c": blk % 2,
    }


def device(at):
    return {
        "blk": ((at["x"] % 2) * 4 + at["y"]) * 2 + at["c"],
        "feat": at["z"] * 2 + at["x"] // 2,
    }


def moved(at, dim, by):
    return {**at, dim: (at[dim] + by) % (2 if dim == "c" else 4)}


class Sender:
    def __init__(self, send_sem, recv_sem):
        self.send_sem, self.recv_sem, self.used, self.all = send_sem, recv_sem, 0, []

    def start(self, ref, to, comes=None):
        i = self.used
        self.used += 1

        def copy_of(ref):
            return pltpu.make_async_remote_copy(
                src_ref=ref,
                dst_ref=ref,
                send_sem=self.send_sem.at[i],
                recv_sem=self.recv_sem.at[i],
                device_id=device(to),
                device_id_type=MESH,
            )

        copy = copy_of(ref)
        self.all.append(copy)
        copy.start()
        return copy if comes is None else copy_of(comes)


N_COPIES = 3 * 50


def first_block(core, span):
    return core * 1024 + span[0] * 64


class Ring:
    def __init__(self, net, me, core, which, full):
        self.net, self.me, self.core, self.which, self.full = net, me, core, which, full
        self.order, self.span = ORDERS[which], COLUMNS[core][which]
        self.size = self.span[1] - self.span[0]
        self.p1, self.p2, self.p3 = (me[d] for d in self.order)
        self.went, self.passed = {}, []

    def place(self, by1, by2, by3):
        at = ((self.p3 + by3) % 4 * 4 + (self.p2 + by2) % 4) * 4 + by1
        return first_block(self.core, self.span) + at * self.size

    def block(self, by1, by2=0, by3=0):
        return self.full.at[pl.ds(self.place((self.p1 + by1) % 4, by2, by3), self.size)]

    def line(self, by3, by2):
        return self.full.at[pl.ds(self.place(0, by2, by3), 4 * self.size)]

    def spread(self, by1):
        for name, by in (("p", 1), ("m", 3)):
            self.send(f"{name}{by1}", self.block(by1), 2, by)
        for name, by in (("u0", 1), ("v0", 3)):
            self.send(f"{name}{by1}", self.block(by1), 3, by)

    def out(self, by2, *bys):
        for by in bys:
            self.send(f"{'u' if by == 1 else 'v'}{by2}", self.line(0, by2), 3, by)

    def send(self, name, ref, step, by):
        to = moved(self.me, self.order[step - 1], by)
        self.went[name] = self.net.start(ref, to)

    def came(self, *names):
        for name in names:
            self.went[name].wait_recv()

    def share(self, by3, by2):
        to = moved(self.me, "c", 1)
        theirs = Ring(self.net, self.me, 1 - self.core, self.which, self.full)
        self.passed.append(self.net.start(self.line(by3, by2), to, theirs.line(by3, by2)))


def gather_kernel(
    x_ref, tiles_hbm, rows_hbm, cols_hbm, full, tiles, codes,
    rows, cols, own_sem, slot_sem, tile_sem, send_sem, recv_sem,
):
    me = place()
    sibling = moved(me, "c", 1)
    neighbours = [moved(me, d, by) for d in "xyz" for by in (1, 3)] + [sibling]
    barrier = pltpu.get_barrier_semaphore()
    for other in neighbours:
        pl.semaphore_signal(barrier, inc=1, device_id=device(other), device_id_type=MESH)
    slot_loads = [
        pltpu.make_async_copy(rows_hbm, rows, slot_sem.at[0]),
        pltpu.make_async_copy(cols_hbm, cols, slot_sem.at[1]),
    ]
    for copy in slot_loads:
        copy.start()
    for core in range(2):
        pl.when(me["c"] == core)(
            functools.partial(
                gather_core, core, me, neighbours, barrier, x_ref, tiles_hbm, full, tiles, codes,
                rows, cols, slot_loads, own_sem, tile_sem, send_sem, recv_sem,
            )
        )


def gather_core(
    core, me, neighbours, barrier, x_ref, tiles_hbm, full, tiles, codes,
    rows, cols, slot_loads, own_sem, tile_sem, send_sem, recv_sem,
):
    net = Sender(send_sem, recv_sem)
    rings = [Ring(net, me, core, which, full) for which in range(3)]
    own = []
    for r in rings:
        for i, ct in enumerate(range(*r.span)):
            own.append(
                pltpu.make_async_copy(
                    x_ref.at[:, ct * TILE : (ct + 1) * TILE],
                    r.full.at[r.place(r.p1, 0, 0) + i],
                    own_sem.at[ct],
                )
            )
            own[-1].start()
    for copy in own:
        copy.wait()
    pl.semaphore_wait(barrier, len(neighbours))

    lower, upper = (slice(None), slice(0, 16)), (slice(None), slice(16, 32))
    for r in rings:
        r.send("a", r.block(0), 1, 1)
        r.send("b", r.block(0), 1, 3)
    for r in rings:
        r.spread(0)
    sources = rows.shape[0]
    slots = tiles_hbm.shape[0] // sources
    loads = []
    for i in range(sources):
        copy = pltpu.make_async_copy(
            tiles_hbm.at[i * slots : i * slots + EARLY],
            tiles.at[i * EARLY : (i + 1) * EARLY],
            tile_sem.at[i],
        )
        loads.append(copy)
        loads[-1].start()
    for copy in slot_loads:
        copy.wait()
    codes[...] = slot_codes(rows[...], cols[...])
    for r in rings:
        r.came("a")
        r.send("af", r.block(3).at[lower], 1, 1)
        r.came("b")
        r.send("bf", r.block(1).at[upper], 1, 3)
    for r in rings:
        r.spread(3)
        r.spread(1)
    for r in rings:
        r.came("p0")
        r.send("pf0", r.block(0, 3), 2, 1)
    for r in rings:
        r.came("af", "bf")
        r.spread(2)
        r.share(0, 0)
    for r in rings:
        r.came("p3")
        r.send("pf3", r.block(3, 3), 2, 1)
        r.came("m1")
        r.send("mf1", r.block(1, 1), 2, 3)
    for r in rings:
        r.came("m0", "m3", "m2")
        r.send("mf2", r.block(2, 1), 2, 3)
        r.out(1, 3)
        r.came("p1", "p2")
        r.out(3, 1, 3)
        r.out(1, 1)
        r.share(0, 1)
        r.share(0, 3)
    for r in rings:
        r.came("u00", "u03", "u01", "u02")
        r.send("u0f", r.line(3, 0), 3, 1)
        r.share(3, 0)
        r.came("v00", "v03", "v01", "v02")
        r.share(1, 0)
    for r in rings:
        r.came("pf0", "pf3", "mf1", "mf2")
        r.out(2, 3, 1)
        r.share(0, 2)
    for name, by3, by2, on in (
        ("v1", 1, 1, 3), ("u3", 3, 3, 1), ("u1", 3, 1, 0), ("v3", 1, 3, 0),
        ("v2", 1, 2, 3), ("u2", 3, 2, 0),
    ):
        for r in rings:
            r.came(name)
            if on:
                r.send(name + "f", r.line(by3, by2), 3, on)
            r.share(by3, by2)
    for name, by2 in (("u0f", 0), ("u3f", 3), ("v1f", 1), ("v2f", 2)):
        for r in rings:
            r.came(name)
            r.share(2, by2)
    for r in rings:
        for copy in r.passed:
            copy.wait_recv()
    for copy in net.all:
        copy.wait_send()
    for copy in loads:
        copy.wait()


def slot_codes(rows, cols):
    source = lax.broadcasted_iota(jnp.int32, rows.shape, 0)
    slot = lax.broadcasted_iota(jnp.int32, rows.shape, 1)
    c, y, x = source & 1, (source >> 1) & 3, source >> 3
    at = {"x": x, "y": y, "z": jnp.zeros_like(x)}
    block, layout = 0, 0
    for core in range(2):
        for i, (dims, span) in enumerate(zip(ORDERS, COLUMNS[core])):
            d1, d2, d3 = (at[d] for d in dims)
            size = span[1] - span[0]
            here = first_block(core, span) + ((d3 * 4 + d2) * 4 + d1) * size + cols - span[0]
            inside = (c == core) & (cols >= span[0])
            block = jnp.where(inside, here, block)
            layout = jnp.where(inside, core * 3 + i, layout)
    tile = source * EARLY + jnp.where(slot < EARLY, slot, slot - EARLY)
    return (tile << 19) | (block << 8) | (layout << 5) | rows


def strides(dim):
    return [
        (hi - lo) * 4 ** dims.index(dim)
        for columns in COLUMNS
        for dims, (lo, hi) in zip(ORDERS, columns)
    ]


def gather(features, tiles, rows, cols):
    hbm = pl.BlockSpec(memory_space=pltpu.HBM)
    vmem = pl.BlockSpec(memory_space=pltpu.VMEM)
    dma = pltpu.SemaphoreType.DMA
    return pl.pallas_call(
        gather_kernel,
        out_shape=(
            pltpu.VMEM((2048, 32, TILE), jnp.bfloat16),
            pltpu.VMEM((tiles.shape[0] // 2, TILE, TILE), jnp.bfloat16),
            jax.ShapeDtypeStruct(rows.shape, jnp.int32),
        ),
        in_specs=[hbm] * 4,
        out_specs=(vmem, vmem, vmem),
        scratch_shapes=[
            pltpu.VMEM(rows.shape, jnp.int32), pltpu.VMEM(cols.shape, jnp.int32),
            dma((16,)), dma((2,)), dma((rows.shape[0],)), dma((N_COPIES,)), dma((N_COPIES,)),
        ],
        compiler_params=pltpu.CompilerParams(
            collective_id=0, has_side_effects=True, vmem_limit_bytes=2 * MIB
        ),
        name="gather",
    )(*(in_hbm(a) for a in (features, tiles, rows, cols)))


BATCH = 32


def aggregate_kernel(
    codes, counts, full, early, tiles_hbm, out_ref,
    late, total, listed, steps_z, steps_x, late_sem,
):
    sources, slots = codes.shape

    def late_copy(s):
        return pltpu.make_async_copy(
            tiles_hbm.at[pl.ds(s * slots + EARLY, EARLY)],
            late.at[pl.ds(s * EARLY, EARLY)],
            late_sem.at[s],
        )

    @pl.loop(0, sources)
    def _(s):
        pl.when(counts[s] > EARLY)(lambda: late_copy(s).start())

    total[...] = jnp.zeros_like(total)

    def enlist(first):
        def enter(s, end):
            live = jnp.clip(counts[s] - first, 0, EARLY)

            def eight(j, carry):
                for u in range(8):
                    listed[end + j * 8 + u] = codes[s, first + j * 8 + u]
                return carry

            lax.fori_loop(0, (live + 7) >> 3, eight, 0)
            return end + live

        end = lax.fori_loop(0, sources, enter, 0)
        for u in range(BATCH):
            listed[end + u] = out_ref.shape[0]
        return (end + BATCH - 1) // BATCH

    for i in range(6):
        steps_z[i] = strides("z")[i]
        steps_x[i] = strides("x")[i] * 2

    def panel(code):
        block, layout = (code >> 8) & 2047, (code >> 5) & 7
        step_z, step_x = steps_z[layout], steps_x[layout]
        parts = [full[block + z * step_z + x_hi * step_x] for z in range(4) for x_hi in range(2)]
        return jnp.concatenate(parts, axis=0)

    def work(steps, tiles):
        @pl.loop(0, steps)
        def _(b):
            for part in range(0, BATCH, BATCH // 2):
                entries = [listed[b * BATCH + part + u] for u in range(BATCH // 2)]
                products = [
                    lax.dot_general(
                        panel(code),
                        tiles[code >> 19],
                        (((1,), (1,)), ((), ())),
                        preferred_element_type=jnp.float32,
                    )
                    for code in entries
                ]
                for code, product in zip(entries, products):
                    total[code & 31] += product

    work(enlist(0), early)

    @pl.loop(0, sources)
    def _(s):
        pl.when(counts[s] > EARLY)(lambda: late_copy(s).wait())

    work(enlist(EARLY), late)
    out_ref[...] = total[: out_ref.shape[0]].astype(out_ref.dtype)


def aggregate(codes, counts, full, early, tiles):
    smem = pl.BlockSpec(memory_space=pltpu.SMEM)
    vmem = pl.BlockSpec(memory_space=pltpu.VMEM)
    return pl.pallas_call(
        aggregate_kernel,
        out_shape=pltpu.VMEM((16, 256, TILE), jnp.bfloat16),
        in_specs=[smem, smem, vmem, vmem, pl.BlockSpec(memory_space=pltpu.HBM)],
        out_specs=vmem,
        scratch_shapes=[
            pltpu.VMEM(early.shape, jnp.bfloat16),
            pltpu.VMEM((17, 256, TILE), jnp.float32),
            pltpu.SMEM((codes.size // 2 + BATCH + 8,), jnp.int32),
            pltpu.SMEM((6,), jnp.int32),
            pltpu.SMEM((6,), jnp.int32),
            pltpu.SemaphoreType.DMA((codes.shape[0],)),
        ],
        compiler_params=pltpu.CompilerParams(vmem_limit_bytes=17 * MIB),
        name="aggregate",
    )(codes, counts, in_vmem(full), in_vmem(early), in_hbm(tiles))


def tail_kernel(
    part, weight, cotangent, act_ref, sums_ref,
    held, terms, terms_in, psem, pin, tsem, tin, msem, min_,
):
    blk, feat = lax.axis_index("blk"), lax.axis_index("feat")
    barrier = pltpu.get_barrier_semaphore()
    for i in range(1, 8):
        pl.semaphore_signal(
            barrier, inc=1, device_id={"feat": (feat + i) % 8}, device_id_type=MESH
        )
    for i in range(1, 16):
        pl.semaphore_signal(
            barrier, inc=1, device_id={"blk": (blk + i) % 16}, device_id_type=MESH
        )
    pl.semaphore_wait(barrier, 22)

    def remote(src, dst, send, recv, to):
        copy = pltpu.make_async_remote_copy(
            src_ref=src, dst_ref=dst, send_sem=send, recv_sem=recv,
            device_id=to, device_id_type=MESH,
        )
        copy.start()
        return copy

    sent = []
    for i in range(1, 8):
        to = (feat + i) % 8
        sent.append(
            remote(part.at[to], held.at[i - 1], psem.at[i - 1], pin.at[i - 1], {"feat": to})
        )
    summed = part[feat].astype(jnp.float32)
    for i in range(7):
        sent[i].wait_recv()
        summed = summed + held[i].astype(jnp.float32)
    nodes = summed.astype(jnp.bfloat16)
    nodes = jnp.concatenate([nodes[0], nodes[1]], axis=1)
    preact = jnp.dot(weight[...], nodes, preferred_element_type=jnp.float32)
    sigmoid = jax.nn.sigmoid(preact)
    act_ref[...] = (preact * sigmoid).astype(jnp.bfloat16)
    slope = cotangent[...].astype(jnp.float32) * sigmoid * (1.0 + preact * (1.0 - sigmoid))
    local = lax.dot_general(
        slope.astype(jnp.bfloat16),
        nodes,
        (((1,), (1,)), ((), ())),
        preferred_element_type=jnp.float32,
    )
    terms[...] = local.reshape(terms.shape).astype(terms.dtype)
    sent_terms = []
    for i in range(1, 8):
        to = (feat + i) % 8
        sent_terms.append(
            remote(terms.at[to], terms_in.at[i - 1], tsem.at[i - 1], tin.at[i - 1], {"feat": to})
        )
    share = terms[feat].astype(jnp.float32)
    for i in range(7):
        sent_terms[i].wait_recv()
        share = share + terms_in[i].astype(jnp.float32)
    sums_ref[blk] = share.astype(sums_ref.dtype)
    sent_sums = []
    for i in range(1, 16):
        sent_sums.append(
            remote(
                sums_ref.at[blk], sums_ref.at[blk], msem.at[i - 1], min_.at[i - 1],
                {"blk": (blk + i) % 16},
            )
        )
    for copy in sent_sums:
        copy.wait_recv()
    for copy in sent + sent_terms + sent_sums:
        copy.wait_send()


def tail(part, weight, cotangent):
    vmem = pl.BlockSpec(memory_space=pltpu.VMEM)
    dma = pltpu.SemaphoreType.DMA
    return pl.pallas_call(
        tail_kernel,
        out_shape=(
            pltpu.VMEM((256, 256), jnp.bfloat16),
            pltpu.VMEM((16, 32, 256), jnp.bfloat16),
        ),
        in_specs=[vmem] * 3,
        out_specs=(vmem, vmem),
        scratch_shapes=[
            pltpu.VMEM((7, 2, 256, TILE), jnp.bfloat16),
            pltpu.VMEM((8, 32, 256), jnp.bfloat16),
            pltpu.VMEM((7, 32, 256), jnp.bfloat16),
            dma((7,)), dma((7,)), dma((7,)), dma((7,)), dma((15,)), dma((15,)),
        ],
        compiler_params=pltpu.CompilerParams(
            collective_id=1, has_side_effects=True, vmem_limit_bytes=10 * MIB
        ),
        name="tail",
    )(in_vmem(part), weight, cotangent)


def finish_kernel(act, sums, act_ref, grad_ref):
    act_ref[...] = act[...]
    grad_ref[...] = jnp.sum(sums[...].astype(jnp.float32), axis=0) * (1.0 / math.sqrt(32768))


def finish(act, sums):
    vmem = pl.BlockSpec(memory_space=pltpu.VMEM)
    return pl.pallas_call(
        finish_kernel,
        out_shape=(
            jax.ShapeDtypeStruct(act.shape, act.dtype),
            jax.ShapeDtypeStruct(sums.shape[1:], jnp.float32),
        ),
        in_specs=[vmem] * 2,
        out_specs=(vmem, vmem),
        name="finish",
    )(in_vmem(act), in_vmem(sums))


def shards(features, adj_tiles, tile_rows, tile_cols, counts, weight, cotangent):
    sources, slots = adj_tiles.shape[2:4]
    tiles = adj_tiles.reshape(sources * slots, TILE, TILE)
    rows, cols = (a.reshape(sources, slots) for a in (tile_rows, tile_cols))
    full, early, codes = gather(features, tiles, rows, cols)
    part = aggregate(codes, counts.reshape(sources), full, early, tiles)
    part = part.reshape(8, 2, 256, TILE)
    return finish(*tail(part, weight, cotangent))


def solution(mesh):
    in_specs = (
        P("feat", "blk"),
        P("blk", "feat", None, None, None, None),
        P("blk", "feat", None, None),
        P("blk", "feat", None, None),
        P("blk", "feat", None),
        P(),
        P(None, ("blk", "feat")),
    )
    out_specs = (P(None, ("blk", "feat")), P("feat", None))
    return jax.shard_map(shards, mesh=mesh, in_specs=in_specs, out_specs=out_specs, check_vma=False)
```

```python
import functools
import math

import jax
import jax.numpy as jnp
from jax import lax
from jax.experimental import pallas as pl
from jax.experimental.pallas import tpu as pltpu
from jax.sharding import PartitionSpec as P

MESH = pl.DeviceIdType.MESH
TILE = 128
ORDERS = (("x", "y", "z"), ("y", "z", "x"), ("z", "x", "y"))
COLUMNS = (((0, 6), (6, 11), (11, 16)), ((0, 5), (5, 11), (11, 16)))
MIB = 2**20


EARLY = 24


def in_vmem(array):
    return pltpu.with_memory_space_constraint(array, pltpu.VMEM)


def in_hbm(array):
    return pltpu.with_memory_space_constraint(array, pltpu.HBM)


def place():
    blk = lax.axis_index("blk")
    feat = lax.axis_index("feat")
    return {
        "x": (feat % 2) * 2 + blk // 8,
        "y": (blk // 2) % 4,
        "z": feat // 2,
        "c": blk % 2,
    }


def device(at):
    return {
        "blk": ((at["x"] % 2) * 4 + at["y"]) * 2 + at["c"],
        "feat": at["z"] * 2 + at["x"] // 2,
    }


def moved(at, dim, by):
    return {**at, dim: (at[dim] + by) % (2 if dim == "c" else 4)}


class Sender:
    def __init__(self, send_sem, recv_sem):
        self.send_sem, self.recv_sem, self.used, self.all = send_sem, recv_sem, 0, []

    def start(self, ref, to, comes=None):
        i = self.used
        self.used += 1

        def copy_of(ref):
            return pltpu.make_async_remote_copy(
                src_ref=ref,
                dst_ref=ref,
                send_sem=self.send_sem.at[i],
                recv_sem=self.recv_sem.at[i],
                device_id=device(to),
                device_id_type=MESH,
            )

        copy = copy_of(ref)
        self.all.append(copy)
        copy.start()
        return copy if comes is None else copy_of(comes)


N_COPIES = 3 * 50


def first_block(core, span):
    return core * 1024 + span[0] * 64


class Ring:
    def __init__(self, net, me, core, which, full):
        self.net, self.me, self.core, self.which, self.full = net, me, core, which, full
        self.order, self.span = ORDERS[which], COLUMNS[core][which]
        self.size = self.span[1] - self.span[0]
        self.p1, self.p2, self.p3 = (me[d] for d in self.order)
        self.went, self.passed = {}, []

    def place(self, by1, by2, by3):
        at = ((self.p3 + by3) % 4 * 4 + (self.p2 + by2) % 4) * 4 + by1
        return first_block(self.core, self.span) + at * self.size

    def block(self, by1, by2=0, by3=0):
        return self.full.at[pl.ds(self.place((self.p1 + by1) % 4, by2, by3), self.size)]

    def line(self, by3, by2):
        return self.full.at[pl.ds(self.place(0, by2, by3), 4 * self.size)]

    def spread(self, by1):
        for name, by in (("p", 1), ("m", 3)):
            self.send(f"{name}{by1}", self.block(by1), 2, by)
        for name, by in (("u0", 1), ("v0", 3)):
            self.send(f"{name}{by1}", self.block(by1), 3, by)

    def out(self, by2, *bys):
        for by in bys:
            self.send(f"{'u' if by == 1 else 'v'}{by2}", self.line(0, by2), 3, by)

    def send(self, name, ref, step, by):
        to = moved(self.me, self.order[step - 1], by)
        self.went[name] = self.net.start(ref, to)

    def came(self, *names):
        for name in names:
            self.went[name].wait_recv()

    def share(self, by3, by2):
        to = moved(self.me, "c", 1)
        theirs = Ring(self.net, self.me, 1 - self.core, self.which, self.full)
        self.passed.append(self.net.start(self.line(by3, by2), to, theirs.line(by3, by2)))


def gather_kernel(
    x_ref, tiles_hbm, rows_hbm, cols_hbm, full, tiles, codes,
    rows, cols, own_sem, slot_sem, tile_sem, send_sem, recv_sem,
):
    me = place()
    sibling = moved(me, "c", 1)
    neighbours = [moved(me, d, by) for d in "xyz" for by in (1, 3)] + [sibling]
    barrier = pltpu.get_barrier_semaphore()
    for other in neighbours:
        pl.semaphore_signal(barrier, inc=1, device_id=device(other), device_id_type=MESH)
    slot_loads = [
        pltpu.make_async_copy(rows_hbm, rows, slot_sem.at[0]),
        pltpu.make_async_copy(cols_hbm, cols, slot_sem.at[1]),
    ]
    for copy in slot_loads:
        copy.start()
    for core in range(2):
        pl.when(me["c"] == core)(
            functools.partial(
                gather_core, core, me, neighbours, barrier, x_ref, tiles_hbm, full, tiles, codes,
                rows, cols, slot_loads, own_sem, tile_sem, send_sem, recv_sem,
            )
        )


def gather_core(
    core, me, neighbours, barrier, x_ref, tiles_hbm, full, tiles, codes,
    rows, cols, slot_loads, own_sem, tile_sem, send_sem, recv_sem,
):
    net = Sender(send_sem, recv_sem)
    rings = [Ring(net, me, core, which, full) for which in range(3)]
    own = []
    for r in rings:
        for i, ct in enumerate(range(*r.span)):
            own.append(
                pltpu.make_async_copy(
                    x_ref.at[:, ct * TILE : (ct + 1) * TILE],
                    r.full.at[r.place(r.p1, 0, 0) + i],
                    own_sem.at[ct],
                )
            )
            own[-1].start()
    for copy in own:
        copy.wait()
    pl.semaphore_wait(barrier, len(neighbours))

    lower, upper = (slice(None), slice(0, 16)), (slice(None), slice(16, 32))
    for r in rings:
        r.send("a", r.block(0), 1, 1)
        r.send("b", r.block(0), 1, 3)
    for r in rings:
        r.spread(0)
    sources = rows.shape[0]
    slots = tiles_hbm.shape[0] // sources
    loads = []
    for i in range(sources):
        copy = pltpu.make_async_copy(
            tiles_hbm.at[i * slots : i * slots + EARLY],
            tiles.at[i * EARLY : (i + 1) * EARLY],
            tile_sem.at[i],
        )
        loads.append(copy)
        loads[-1].start()
    for copy in slot_loads:
        copy.wait()
    codes[...] = slot_codes(rows[...], cols[...])
    for r in rings:
        r.came("a")
        r.send("af", r.block(3).at[lower], 1, 1)
        r.came("b")
        r.send("bf", r.block(1).at[upper], 1, 3)
    for r in rings:
        r.spread(3)
        r.spread(1)
    for r in rings:
        r.came("p0")
        r.send("pf0", r.block(0, 3), 2, 1)
    for r in rings:
        r.came("af", "bf")
        r.spread(2)
        r.share(0, 0)
    for r in rings:
        r.came("p3")
        r.send("pf3", r.block(3, 3), 2, 1)
        r.came("m1")
        r.send("mf1", r.block(1, 1), 2, 3)
    for r in rings:
        r.came("m0", "m3", "m2")
        r.send("mf2", r.block(2, 1), 2, 3)
        r.out(1, 3)
        r.came("p1", "p2")
        r.out(3, 1, 3)
        r.out(1, 1)
        r.share(0, 1)
        r.share(0, 3)
    for r in rings:
        r.came("u00", "u03", "u01", "u02")
        r.send("u0f", r.line(3, 0), 3, 1)
        r.share(3, 0)
        r.came("v00", "v03", "v01", "v02")
        r.share(1, 0)
    for r in rings:
        r.came("pf0", "pf3", "mf1", "mf2")
        r.out(2, 3, 1)
        r.share(0, 2)
    for name, by3, by2, on in (
        ("v1", 1, 1, 3), ("u3", 3, 3, 1), ("u1", 3, 1, 0), ("v3", 1, 3, 0),
        ("v2", 1, 2, 3), ("u2", 3, 2, 0),
    ):
        for r in rings:
            r.came(name)
            if on:
                r.send(name + "f", r.line(by3, by2), 3, on)
            r.share(by3, by2)
    for name, by2 in (("u0f", 0), ("u3f", 3), ("v1f", 1), ("v2f", 2)):
        for r in rings:
            r.came(name)
            r.share(2, by2)
    for r in rings:
        for copy in r.passed:
            copy.wait_recv()
    for copy in net.all:
        copy.wait_send()
    for copy in loads:
        copy.wait()


def slot_codes(rows, cols):
    source = lax.broadcasted_iota(jnp.int32, rows.shape, 0)
    slot = lax.broadcasted_iota(jnp.int32, rows.shape, 1)
    c, y, x = source & 1, (source >> 1) & 3, source >> 3
    at = {"x": x, "y": y, "z": jnp.zeros_like(x)}
    block, layout = 0, 0
    for core in range(2):
        for i, (dims, span) in enumerate(zip(ORDERS, COLUMNS[core])):
            d1, d2, d3 = (at[d] for d in dims)
            size = span[1] - span[0]
            here = first_block(core, span) + ((d3 * 4 + d2) * 4 + d1) * size + cols - span[0]
            inside = (c == core) & (cols >= span[0])
            block = jnp.where(inside, here, block)
            layout = jnp.where(inside, core * 3 + i, layout)
    tile = source * EARLY + jnp.where(slot < EARLY, slot, slot - EARLY)
    return (tile << 19) | (block << 8) | (layout << 5) | rows


def strides(dim):
    return [
        (hi - lo) * 4 ** dims.index(dim)
        for columns in COLUMNS
        for dims, (lo, hi) in zip(ORDERS, columns)
    ]


def gather(features, tiles, rows, cols):
    hbm = pl.BlockSpec(memory_space=pltpu.HBM)
    vmem = pl.BlockSpec(memory_space=pltpu.VMEM)
    dma = pltpu.SemaphoreType.DMA
    return pl.pallas_call(
        gather_kernel,
        out_shape=(
            pltpu.VMEM((2048, 32, TILE), jnp.bfloat16),
            pltpu.VMEM((tiles.shape[0] // 2, TILE, TILE), jnp.bfloat16),
            jax.ShapeDtypeStruct(rows.shape, jnp.int32),
        ),
        in_specs=[hbm] * 4,
        out_specs=(vmem, vmem, vmem),
        scratch_shapes=[
            pltpu.VMEM(rows.shape, jnp.int32), pltpu.VMEM(cols.shape, jnp.int32),
            dma((16,)), dma((2,)), dma((rows.shape[0],)), dma((N_COPIES,)), dma((N_COPIES,)),
        ],
        compiler_params=pltpu.CompilerParams(
            collective_id=0, has_side_effects=True, vmem_limit_bytes=2 * MIB
        ),
        name="gather",
    )(*(in_hbm(a) for a in (features, tiles, rows, cols)))


BATCH = 32


def aggregate_kernel(
    codes, counts, full, early, tiles_hbm, out_ref,
    late, total, listed, steps_z, steps_x, late_sem,
):
    sources, slots = codes.shape

    def late_copy(s):
        return pltpu.make_async_copy(
            tiles_hbm.at[pl.ds(s * slots + EARLY, EARLY)],
            late.at[pl.ds(s * EARLY, EARLY)],
            late_sem.at[s],
        )

    @pl.loop(0, sources)
    def _(s):
        pl.when(counts[s] > EARLY)(lambda: late_copy(s).start())

    total[...] = jnp.zeros_like(total)

    def enlist(first):
        def enter(s, end):
            live = jnp.clip(counts[s] - first, 0, EARLY)

            def eight(j, carry):
                for u in range(8):
                    listed[end + j * 8 + u] = codes[s, first + j * 8 + u]
                return carry

            lax.fori_loop(0, (live + 7) >> 3, eight, 0)
            return end + live

        end = lax.fori_loop(0, sources, enter, 0)
        for u in range(BATCH):
            listed[end + u] = out_ref.shape[0]
        return (end + BATCH - 1) // BATCH

    for i in range(6):
        steps_z[i] = strides("z")[i]
        steps_x[i] = strides("x")[i] * 2

    def panel(code):
        block, layout = (code >> 8) & 2047, (code >> 5) & 7
        step_z, step_x = steps_z[layout], steps_x[layout]
        parts = [full[block + z * step_z + x_hi * step_x] for z in range(4) for x_hi in range(2)]
        return jnp.concatenate(parts, axis=0)

    def work(steps, tiles):
        @pl.loop(0, steps)
        def _(b):
            for part in range(0, BATCH, BATCH // 2):
                entries = [listed[b * BATCH + part + u] for u in range(BATCH // 2)]
                products = [
                    lax.dot_general(
                        panel(code),
                        tiles[code >> 19],
                        (((1,), (1,)), ((), ())),
                        preferred_element_type=jnp.float32,
                    )
                    for code in entries
                ]
                for code, product in zip(entries, products):
                    total[code & 31] += product

    work(enlist(0), early)

    @pl.loop(0, sources)
    def _(s):
        pl.when(counts[s] > EARLY)(lambda: late_copy(s).wait())

    work(enlist(EARLY), late)
    out_ref[...] = total[: out_ref.shape[0]].astype(out_ref.dtype)


def aggregate(codes, counts, full, early, tiles):
    smem = pl.BlockSpec(memory_space=pltpu.SMEM)
    vmem = pl.BlockSpec(memory_space=pltpu.VMEM)
    return pl.pallas_call(
        aggregate_kernel,
        out_shape=pltpu.VMEM((16, 256, TILE), jnp.bfloat16),
        in_specs=[smem, smem, vmem, vmem, pl.BlockSpec(memory_space=pltpu.HBM)],
        out_specs=vmem,
        scratch_shapes=[
            pltpu.VMEM(early.shape, jnp.bfloat16),
            pltpu.VMEM((17, 256, TILE), jnp.float32),
            pltpu.SMEM((codes.size // 2 + BATCH + 8,), jnp.int32),
            pltpu.SMEM((6,), jnp.int32),
            pltpu.SMEM((6,), jnp.int32),
            pltpu.SemaphoreType.DMA((codes.shape[0],)),
        ],
        compiler_params=pltpu.CompilerParams(vmem_limit_bytes=17 * MIB),
        name="aggregate",
    )(codes, counts, in_vmem(full), in_vmem(early), in_hbm(tiles))


def tail_kernel(
    part, weight, cotangent, act_ref, sums_ref,
    held, terms, terms_in, psem, pin, tsem, tin, msem, min_,
):
    blk, feat = lax.axis_index("blk"), lax.axis_index("feat")
    barrier = pltpu.get_barrier_semaphore()
    for i in range(1, 8):
        pl.semaphore_signal(
            barrier, inc=1, device_id={"feat": (feat + i) % 8}, device_id_type=MESH
        )
    for i in range(1, 16):
        pl.semaphore_signal(
            barrier, inc=1, device_id={"blk": (blk + i) % 16}, device_id_type=MESH
        )
    pl.semaphore_wait(barrier, 22)

    def remote(src, dst, send, recv, to):
        copy = pltpu.make_async_remote_copy(
            src_ref=src, dst_ref=dst, send_sem=send, recv_sem=recv,
            device_id=to, device_id_type=MESH,
        )
        copy.start()
        return copy

    sent = [None] * 7
    for i in (5, 3, 4, 1, 7, 2, 6):
        to = (feat + i) % 8
        sent[i - 1] = remote(
            part.at[to], held.at[i - 1], psem.at[i - 1], pin.at[i - 1], {"feat": to}
        )
    summed = part[feat].astype(jnp.float32)
    for i in (1, 5, 0, 6, 2, 3, 4):
        sent[i].wait_recv()
        summed = summed + held[i].astype(jnp.float32)
    nodes = summed.astype(jnp.bfloat16)
    nodes = jnp.concatenate([nodes[0], nodes[1]], axis=1)
    preact = jnp.dot(weight[...], nodes, preferred_element_type=jnp.float32)
    sigmoid = jax.nn.sigmoid(preact)
    act_ref[...] = (preact * sigmoid).astype(jnp.bfloat16)
    slope = cotangent[...].astype(jnp.float32) * sigmoid * (1.0 + preact * (1.0 - sigmoid))
    local = lax.dot_general(
        slope.astype(jnp.bfloat16),
        nodes,
        (((1,), (1,)), ((), ())),
        preferred_element_type=jnp.float32,
    )
    terms[...] = local.reshape(terms.shape).astype(terms.dtype)
    sent_terms = []
    for i in range(1, 8):
        to = (feat + i) % 8
        sent_terms.append(
            remote(terms.at[to], terms_in.at[i - 1], tsem.at[i - 1], tin.at[i - 1], {"feat": to})
        )
    share = terms[feat].astype(jnp.float32)
    for i in range(7):
        sent_terms[i].wait_recv()
        share = share + terms_in[i].astype(jnp.float32)
    sums_ref[blk] = share.astype(sums_ref.dtype)
    sent_sums = []
    for i in range(1, 16):
        sent_sums.append(
            remote(
                sums_ref.at[blk], sums_ref.at[blk], msem.at[i - 1], min_.at[i - 1],
                {"blk": (blk + i) % 16},
            )
        )
    for copy in sent_sums:
        copy.wait_recv()
    for copy in sent + sent_terms + sent_sums:
        copy.wait_send()


def tail(part, weight, cotangent):
    vmem = pl.BlockSpec(memory_space=pltpu.VMEM)
    dma = pltpu.SemaphoreType.DMA
    return pl.pallas_call(
        tail_kernel,
        out_shape=(
            pltpu.VMEM((256, 256), jnp.bfloat16),
            pltpu.VMEM((16, 32, 256), jnp.bfloat16),
        ),
        in_specs=[vmem] * 3,
        out_specs=(vmem, vmem),
        scratch_shapes=[
            pltpu.VMEM((7, 2, 256, TILE), jnp.bfloat16),
            pltpu.VMEM((8, 32, 256), jnp.bfloat16),
            pltpu.VMEM((7, 32, 256), jnp.bfloat16),
            dma((7,)), dma((7,)), dma((7,)), dma((7,)), dma((15,)), dma((15,)),
        ],
        compiler_params=pltpu.CompilerParams(
            collective_id=1, has_side_effects=True, vmem_limit_bytes=10 * MIB
        ),
        name="tail",
    )(in_vmem(part), weight, cotangent)


def finish_kernel(act, sums, act_ref, grad_ref):
    act_ref[...] = act[...]
    grad_ref[...] = jnp.sum(sums[...].astype(jnp.float32), axis=0) * (1.0 / math.sqrt(32768))


def finish(act, sums):
    vmem = pl.BlockSpec(memory_space=pltpu.VMEM)
    return pl.pallas_call(
        finish_kernel,
        out_shape=(
            jax.ShapeDtypeStruct(act.shape, act.dtype),
            jax.ShapeDtypeStruct(sums.shape[1:], jnp.float32),
        ),
        in_specs=[vmem] * 2,
        out_specs=(vmem, vmem),
        name="finish",
    )(in_vmem(act), in_vmem(sums))


def shards(features, adj_tiles, tile_rows, tile_cols, counts, weight, cotangent):
    sources, slots = adj_tiles.shape[2:4]
    tiles = adj_tiles.reshape(sources * slots, TILE, TILE)
    rows, cols = (a.reshape(sources, slots) for a in (tile_rows, tile_cols))
    full, early, codes = gather(features, tiles, rows, cols)
    part = aggregate(codes, counts.reshape(sources), full, early, tiles)
    part = part.reshape(8, 2, 256, TILE)
    return finish(*tail(part, weight, cotangent))


def solution(mesh):
    in_specs = (
        P("feat", "blk"),
        P("blk", "feat", None, None, None, None),
        P("blk", "feat", None, None),
        P("blk", "feat", None, None),
        P("blk", "feat", None),
        P(),
        P(None, ("blk", "feat")),
    )
    out_specs = (P(None, ("blk", "feat")), P("feat", None))
    return jax.shard_map(shards, mesh=mesh, in_specs=in_specs, out_specs=out_specs, check_vma=False)
```
